512 devices in a mesh: ctx: 64 (over x, z), head: 8 (over y, core).
Axes of the slice: x: 4, y: 4, z: 16, core: 2. Of those that a mesh axis runs over, the one named last changes fastest.
Arguments:
- queries: bfloat16 [12288, 6144], P(('ctx', 'head')), may hold values from -9 to 9
- noisy_token_keys: bfloat16 [12288, 1024], P(('ctx', 'head')), may hold values from -9 to 9
- noisy_token_values: bfloat16 [12288, 1024], P(('ctx', 'head')), may hold values from -6 to 6
- clean_token_keys: bfloat16 [4096, 1024], P(('ctx', 'head')), may hold values from -9 to 9
- clean_token_values: bfloat16 [4096, 1024], P(('ctx', 'head')), may hold values from -6 to 6
- output_gradient: bfloat16 [12288, 6144], P(('ctx', 'head')), may hold values from -6 to 6
- history_list: int32 [64, 64], replicated, may hold values from -1 to 1, as said below
Outputs:
- attn_out: bfloat16 [12288, 6144], P(('ctx', 'head'))
- grad_query: bfloat16 [12288, 6144], P(('ctx', 'head'))
- noisy_key_gradient: bfloat16 [12288, 1024], P(('ctx', 'head'))
- noisy_value_gradient: bfloat16 [12288, 1024], P(('ctx', 'head'))
- grad_key_clean: bfloat16 [4096, 1024], P(('ctx', 'head'))
- grad_value_clean: bfloat16 [4096, 1024], P(('ctx', 'head'))
The draws below stay inside these ranges and needn't reach their ends.
Inputs may be any that keep to these rules, and one draw needn't show every extreme that they name: history_list[d, s] is -1 or a block number below 2; it is -1 unless floor(s / 2) < floor(d / 2); each row has at most 62 entries that are not -1, and some row has exactly 62.
All inputs are finite; a program needn't handle non-finite values.
Results may differ from the reference program's by a relative error of at most 0.018.
Values may be sent and summed in bfloat16 or wider, within the bound.
A program may use at most 64 MiB of HBM per device.

```python
import jax
import jax.numpy as jnp
from jax import lax

QUERY_HEADS = 48
KEY_VALUE_HEADS = 8
HEAD_SIZE = 128
GROUP_QUERY_TOKS = 192
NB = 2
BLK = 32
QDEV = 64
MAXS = 62
NOISY_TOKENS = 12288
CLEAN_TOKENS = 4096
N_CTX = 64


def drawn_pair(key):
    queries_raw = jnp.clip(1.5 * jax.random.normal(jax.random.fold_in(key, 101), (NOISY_TOKENS, QUERY_HEADS * HEAD_SIZE), jnp.float32), -9.0, 9.0)
    unshaped_keys = jnp.clip(1.5 * jax.random.normal(jax.random.fold_in(key, 202), (NOISY_TOKENS, KEY_VALUE_HEADS * HEAD_SIZE), jnp.float32), -9.0, 9.0)
    return (queries_raw, unshaped_keys)


def draw_queries(key, part):
    return drawn_pair(key)[0].astype(jnp.bfloat16)


def draw_noisy_token_keys(key, part):
    return drawn_pair(key)[1].astype(jnp.bfloat16)


def draw_history_list(key, part):
    row_ids = jnp.arange(QDEV, dtype=jnp.int32)
    allowed = (row_ids // 2)[None, :] < (row_ids // 2)[:, None]
    allowed_count = jnp.sum(allowed.astype(jnp.int32), 1)
    wanted = jax.random.randint(jax.random.fold_in(key, 1), (QDEV,), MAXS // 2, MAXS + 1, dtype=jnp.int32)
    wanted = jnp.where(row_ids == QDEV - 1, MAXS, wanted)
    wanted = jnp.minimum(wanted, allowed_count)
    priority = jax.random.randint(jax.random.fold_in(key, 2), (QDEV, QDEV), 0, 2 ** 20, dtype=jnp.int32) * QDEV + row_ids[None, :]
    priority = jnp.where(allowed, priority, 2 ** 30 + row_ids[None, :])
    ranking = jnp.argsort(jnp.argsort(priority, axis=1), axis=1).astype(jnp.int32)
    selected = allowed & (ranking < wanted[:, None])
    block_pick = jax.random.randint(jax.random.fold_in(key, 3), (QDEV, QDEV), 0, NB, dtype=jnp.int32)
    return jnp.where(selected, block_pick, -1).astype(jnp.int32)


def block_scale(own_key, extent, shards, low, high):
    def one(dim, blocks):
        heights = jax.random.uniform(jax.random.fold_in(jax.random.fold_in(own_key, 6), dim), (blocks,), jnp.float32, low / len(shards), high / len(shards))
        return jnp.repeat(jnp.exp(heights), extent[dim] // blocks).reshape((-1,) + (1,) * (len(extent) - dim - 1))

    loudness = one(*shards[0])
    for cut in shards[1:]:
        loudness = loudness * one(*cut)
    return loudness


def gaussian(rng, extent, spread, limit, shards=(), kind=jnp.bfloat16):
    entries = spread * jax.random.normal(rng, extent, jnp.float32)
    if shards:
        entries = entries * block_scale(rng, extent, shards, -0.22, 0.18)
    return jnp.clip(entries, -limit, limit).astype(kind)


def setup_inputs(seed: int = 0) -> dict:
    arg_keys = jax.random.split(jax.random.key(seed), 8)
    return {
        "queries": draw_queries(jax.random.fold_in(arg_keys[7], 71), 0),
        "noisy_token_keys": draw_noisy_token_keys(jax.random.fold_in(arg_keys[7], 71), 0),
        "noisy_token_values": gaussian(arg_keys[2], (NOISY_TOKENS, KEY_VALUE_HEADS * HEAD_SIZE), 1.0, 6.0, ((0, 512),)),
        "clean_token_keys": gaussian(arg_keys[3], (CLEAN_TOKENS, KEY_VALUE_HEADS * HEAD_SIZE), 1.5, 9.0, ((0, 512),)),
        "clean_token_values": gaussian(arg_keys[4], (CLEAN_TOKENS, KEY_VALUE_HEADS * HEAD_SIZE), 1.0, 6.0, ((0, 512),)),
        "output_gradient": gaussian(arg_keys[5], (NOISY_TOKENS, QUERY_HEADS * HEAD_SIZE), 1.0, 6.0, ((0, 512),)),
        "history_list": draw_history_list(jax.random.fold_in(arg_keys[7], 71), 0),
    }


NEG_FILL = -1.0e30


def rounded(values):
    return lax.optimization_barrier(values.astype(jnp.bfloat16)).astype(jnp.float32)


def reference(queries, noisy_token_keys, noisy_token_values, clean_token_keys, clean_token_values, output_gradient, history_list):
    heads_per_group = QUERY_HEADS // KEY_VALUE_HEADS
    logit_scale = HEAD_SIZE ** -0.5
    block_offsets = jnp.arange(BLK, dtype=jnp.int32)

    def one_group(running, query_group_index):
        clean_key_grad, clean_value_grad = running
        query_matrix_rows = lax.dynamic_slice_in_dim(queries, query_group_index * GROUP_QUERY_TOKS, GROUP_QUERY_TOKS, 0).astype(jnp.float32).reshape(GROUP_QUERY_TOKS, KEY_VALUE_HEADS, heads_per_group, HEAD_SIZE)
        incoming_gradient = lax.dynamic_slice_in_dim(output_gradient, query_group_index * GROUP_QUERY_TOKS, GROUP_QUERY_TOKS, 0).astype(jnp.float32).reshape(GROUP_QUERY_TOKS, KEY_VALUE_HEADS, heads_per_group, HEAD_SIZE)
        span_begin_index = (query_group_index // 2) * (2 * GROUP_QUERY_TOKS)
        keys_in_span = lax.dynamic_slice_in_dim(noisy_token_keys, span_begin_index, 2 * GROUP_QUERY_TOKS, 0).astype(jnp.float32).reshape(2 * GROUP_QUERY_TOKS, KEY_VALUE_HEADS, HEAD_SIZE)
        values_in_span = lax.dynamic_slice_in_dim(noisy_token_values, span_begin_index, 2 * GROUP_QUERY_TOKS, 0).astype(jnp.float32).reshape(2 * GROUP_QUERY_TOKS, KEY_VALUE_HEADS, HEAD_SIZE)
        listed = history_list[query_group_index]
        slot_order = jnp.argsort((listed < 0).astype(jnp.int32), stable=True)[:MAXS].astype(jnp.int32)
        chosen = listed[slot_order]
        chosen_live = chosen >= 0
        query_row_index = ((slot_order * NB + jnp.maximum(chosen, 0)) * BLK)[:, None] + block_offsets[None, :]
        query_row_index = query_row_index.reshape(-1).astype(jnp.int32)
        clean_history_keys = clean_token_keys[query_row_index].astype(jnp.float32).reshape(-1, KEY_VALUE_HEADS, HEAD_SIZE)
        clean_history_values = clean_token_values[query_row_index].astype(jnp.float32).reshape(-1, KEY_VALUE_HEADS, HEAD_SIZE)
        all_keys = jnp.concatenate([keys_in_span, clean_history_keys], 0)
        all_values = jnp.concatenate([values_in_span, clean_history_values], 0)
        live_keys = jnp.concatenate([jnp.ones((2 * GROUP_QUERY_TOKS,), jnp.bool_), jnp.repeat(chosen_live, BLK)], 0)
        scores = jnp.einsum('qgrd,kgd->gqrk', query_matrix_rows, all_keys) * logit_scale
        scores = jnp.where(live_keys, scores, NEG_FILL)
        row_max = jnp.max(scores, -1, keepdims=True)
        log_total = row_max + jnp.log(jnp.sum(jnp.exp(scores - row_max), -1, keepdims=True))
        probabilities = jnp.exp(scores - log_total)
        softmax_weights = rounded(probabilities)
        attended = jnp.einsum('gqrk,kgd->qgrd', softmax_weights, all_values).astype(jnp.bfloat16)
        row_dot = jnp.sum(incoming_gradient * attended.astype(jnp.float32), -1).transpose(1, 0, 2)[..., None]
        dprobs = jnp.einsum('qgrd,kgd->gqrk', incoming_gradient, all_values)
        score_gradient = rounded(probabilities * (dprobs - row_dot))
        query_grad = (logit_scale * jnp.einsum('gqrk,kgd->qgrd', score_gradient, all_keys)).astype(jnp.bfloat16)
        key_gradient_terms = (logit_scale * jnp.einsum('xtlv,txlh->vxh', score_gradient, query_matrix_rows)).reshape(-1, KEY_VALUE_HEADS * HEAD_SIZE)
        value_gradient_terms = jnp.einsum('xtlv,txlh->vxh', softmax_weights, incoming_gradient).reshape(-1, KEY_VALUE_HEADS * HEAD_SIZE)
        clean_key_grad = clean_key_grad.at[query_row_index].add(key_gradient_terms[2 * GROUP_QUERY_TOKS:])
        clean_value_grad = clean_value_grad.at[query_row_index].add(value_gradient_terms[2 * GROUP_QUERY_TOKS:])
        produced = (attended.reshape(GROUP_QUERY_TOKS, QUERY_HEADS * HEAD_SIZE), query_grad.reshape(GROUP_QUERY_TOKS, QUERY_HEADS * HEAD_SIZE), key_gradient_terms[:2 * GROUP_QUERY_TOKS], value_gradient_terms[:2 * GROUP_QUERY_TOKS])
        return (clean_key_grad, clean_value_grad), produced

    initial_gradients = jnp.zeros((CLEAN_TOKENS, KEY_VALUE_HEADS * HEAD_SIZE), jnp.float32)
    finals, produced = lax.scan(one_group, (initial_gradients, initial_gradients), jnp.arange(N_CTX, dtype=jnp.int32))
    attended_all, query_grads, key_segments, value_segments = produced
    attn_out = attended_all.reshape(NOISY_TOKENS, QUERY_HEADS * HEAD_SIZE)
    grad_query = query_grads.reshape(NOISY_TOKENS, QUERY_HEADS * HEAD_SIZE)
    noisy_key_gradient = key_segments.reshape(N_CTX // 2, 2, 2 * GROUP_QUERY_TOKS, KEY_VALUE_HEADS * HEAD_SIZE).sum(1).reshape(NOISY_TOKENS, KEY_VALUE_HEADS * HEAD_SIZE).astype(jnp.bfloat16)
    noisy_value_gradient = value_segments.reshape(N_CTX // 2, 2, 2 * GROUP_QUERY_TOKS, KEY_VALUE_HEADS * HEAD_SIZE).sum(1).reshape(NOISY_TOKENS, KEY_VALUE_HEADS * HEAD_SIZE).astype(jnp.bfloat16)
    return (attn_out, grad_query, noisy_key_gradient, noisy_value_gradient, finals[0].astype(jnp.bfloat16), finals[1].astype(jnp.bfloat16))
```

```python
import functools

import jax
import jax.numpy as jnp
from jax import lax
from jax.experimental import pallas as pl
from jax.experimental.pallas import tpu as pltpu
from jax.sharding import PartitionSpec as P

BLK = 32
HEAD_SIZE = 128
SCALE = HEAD_SIZE**-0.5
LOG2E = 1.4426950408889634
NX = 4
F32 = jnp.float32
BF16 = jnp.bfloat16
MESH = pl.DeviceIdType.MESH
ANY = pl.BlockSpec(memory_space=pl.ANY)
VMEM = pl.BlockSpec(memory_space=pltpu.VMEM)
SMEM = pl.BlockSpec(memory_space=pltpu.SMEM)


class Place:
    def __init__(self, nz, nh):
        self.nz, self.nh = nz, nh
        ctx = lax.axis_index("ctx")
        self.head = lax.axis_index("head")
        self.x = ctx // nz
        self.z = ctx % nz
        self.right = nz // 2
        self.left = nz - 1 - nz // 2

    def wrap_x(self, d):
        return lax.rem(self.x + (d + NX), NX)

    def wrap_z(self, d):
        return lax.rem(self.z + (d + self.nz), self.nz)

    def wrap_head(self, d):
        return lax.rem(self.head + (d + self.nh), self.nh)

    def at(self, x, z, head):
        return (x * self.nz + z, head)

    def x_peer(self, d):
        return self.at(self.wrap_x(d), self.z, self.head)

    def z_peer(self, d):
        return self.at(self.x, self.wrap_z(d), self.head)

    def head_peer(self, d):
        return self.at(self.x, self.z, self.wrap_head(d))

    def partner_z(self):
        return self.z + 1 - 2 * lax.rem(self.z, 2)

    def partner(self, head):
        return self.at(self.x, self.partner_z(), head)


def greet(peers):
    barrier = pltpu.get_barrier_semaphore()
    for peer in peers:
        pl.semaphore_signal(barrier, inc=1, device_id=peer, device_id_type=MESH)
    pl.semaphore_wait(barrier, len(peers))


def remote(src, dst, send, recv, peer):
    return pltpu.make_async_remote_copy(
        src_ref=src, dst_ref=dst, send_sem=send, recv_sem=recv, device_id=peer, device_id_type=MESH
    )


def lanes(index, width):
    return pl.ds(pl.multiple_of(index * width, 128), width)


def gather_kernel(
    nz, nh, q, do, k, v, ck, cv, qg, dog, kn, vn, kv_out,
    kv, own_q, own_do, own_k, own_v,
    in_send, in_recv, own_sem, opp_sem, z_send, z_recv, x_send, x_recv, out_sem,
):
    me = Place(nz, nh)
    qw = q.shape[1] // nh
    kw = k.shape[1] // nh
    mine = me.head
    greet(
        [me.head_peer(d) for d in range(1, nh)]
        + [me.partner(me.wrap_head(d)) for d in range(nh)]
        + [me.z_peer(1), me.z_peer(-1), me.x_peer(1), me.x_peer(-1), me.x_peer(2)]
    )
    sends = []

    def go(copy):
        copy.start()
        sends.append(copy)
        return copy

    local = [
        pltpu.make_async_copy(ck.at[:, lanes(mine, kw)], kv.at[me.x, me.z, 0, mine], own_sem.at[0]),
        pltpu.make_async_copy(cv.at[:, lanes(mine, kw)], kv.at[me.x, me.z, 1, mine], own_sem.at[1]),
        pltpu.make_async_copy(k.at[:, lanes(mine, kw)], own_k, own_sem.at[2]),
        pltpu.make_async_copy(v.at[:, lanes(mine, kw)], own_v, own_sem.at[3]),
        pltpu.make_async_copy(q.at[:, lanes(mine, qw)], own_q, own_sem.at[4]),
        pltpu.make_async_copy(do.at[:, lanes(mine, qw)], own_do, own_sem.at[5]),
    ]
    for copy in local:
        copy.start()
    clean = []
    for d in range(1, nh):
        peer, to = me.head_peer(d), me.wrap_head(d)
        for i, src in enumerate((ck, cv)):
            clean.append(
                go(
                    remote(
                        src.at[:, lanes(to, kw)], kv.at[me.x, me.z, i, mine],
                        in_send.at[i, d], in_recv.at[i, d], peer,
                    )
                )
            )
    heads = []
    for d in range(nh):
        to = me.wrap_head(d)
        for i, (src, dst) in enumerate(((k, kn), (v, vn))):
            if d:
                heads.append(
                    go(
                        remote(
                            src.at[:, lanes(to, kw)], dst.at[0, mine],
                            in_send.at[2 + i, d], in_recv.at[2 + i, d], me.head_peer(d),
                        )
                    )
                )
            heads.append(
                go(
                    remote(
                        src.at[:, lanes(to, kw)], dst.at[1, mine],
                        in_send.at[4 + i, d], in_recv.at[4 + i, d], me.partner(to),
                    )
                )
            )
    for i, (src, dst) in enumerate(((q, qg), (do, dog))):
        for d in range(1, nh):
            to = me.wrap_head(d)
            heads.append(
                go(
                    remote(
                        src.at[:, lanes(to, qw)], dst.at[mine],
                        in_send.at[6 + i, d], in_recv.at[6 + i, d], me.head_peer(d),
                    )
                )
            )
    for copy in local[:2]:
        copy.wait()
    for copy in clean:
        copy.wait_recv()

    opposite = me.wrap_x(2)
    mine_unit = kv.at[me.x, me.z]
    first_opp = go(remote(mine_unit, mine_unit, opp_sem.at[0], opp_sem.at[1], me.x_peer(2)))
    columns = (me.x, opposite)
    sideways = []

    def pass_on(z, slot):
        for i, d in enumerate((1, -1)):
            sideways.append(
                go(remote(kv.at[me.x, z], kv.at[me.x, z], x_send.at[i, slot], x_recv.at[i, slot], me.x_peer(d)))
            )

    def hop(direction, unit, step):
        z = me.wrap_z(-step if direction == 0 else step)
        ref = kv.at[columns[unit], z]
        return go(
            remote(
                ref, ref, z_send.at[direction, unit, step], z_recv.at[direction, unit, step],
                me.z_peer(1 if direction == 0 else -1),
            )
        )

    steps = (me.right, me.left)
    flying = {}
    for step in range(max(steps) + 1):
        for unit in (0, 1):
            if step == 0 and unit == 1:
                first_opp.wait_recv()
            for direction in (0, 1):
                if step > 0 and step - 1 < steps[direction]:
                    flying[direction, unit].wait_recv()
                if step < steps[direction]:
                    flying[direction, unit] = hop(direction, unit, step)
            if unit == 0:
                if step == 0:
                    pass_on(me.z, 0)
                else:
                    for direction in (0, 1):
                        if step - 1 < steps[direction]:
                            z = me.wrap_z(-step if direction == 0 else step)
                            pass_on(z, step if direction == 0 else me.right + step)
        if step == 1:
            for copy in local[2:]:
                copy.wait()
            back = [
                pltpu.make_async_copy(own_k, kn.at[0, mine], own_sem.at[0]),
                pltpu.make_async_copy(own_v, vn.at[0, mine], own_sem.at[1]),
                pltpu.make_async_copy(own_q, qg.at[mine], own_sem.at[2]),
                pltpu.make_async_copy(own_do, dog.at[mine], own_sem.at[3]),
            ]
            for copy in back:
                copy.start()
    outs = [
        pltpu.make_async_copy(kv.at[x], kv_out.at[x], out_sem.at[i]) for i, x in enumerate(columns)
    ]
    for copy in outs:
        copy.start()
    for copy in sideways:
        copy.wait_recv()
    for i, d in enumerate((1, -1)):
        x = me.wrap_x(d)
        outs.append(pltpu.make_async_copy(kv.at[x], kv_out.at[x], out_sem.at[2 + i]))
        outs[-1].start()
    for copy in heads:
        copy.wait_recv()
    for copy in sends:
        copy.wait_send()
    for copy in back + outs:
        copy.wait()


def gather(nz, nh, q, do, k, v, ck, cv):
    rows, qw, kw, crows = q.shape[0], q.shape[1] // nh, k.shape[1] // nh, ck.shape[0]
    dma = pltpu.SemaphoreType.DMA
    return pl.pallas_call(
        functools.partial(gather_kernel, nz, nh),
        out_shape=(
            jax.ShapeDtypeStruct((nh, rows, qw), BF16),
            jax.ShapeDtypeStruct((nh, rows, qw), BF16),
            jax.ShapeDtypeStruct((2, nh, rows, kw), BF16),
            jax.ShapeDtypeStruct((2, nh, rows, kw), BF16),
            jax.ShapeDtypeStruct((NX, nz, 2, nh, crows, kw), BF16),
        ),
        in_specs=[ANY] * 6,
        out_specs=(ANY,) * 5,
        scratch_shapes=[
            pltpu.VMEM((NX, nz, 2, nh, crows, kw), BF16),
            pltpu.VMEM((rows, qw), BF16),
            pltpu.VMEM((rows, qw), BF16),
            pltpu.VMEM((rows, kw), BF16),
            pltpu.VMEM((rows, kw), BF16),
            dma((8, nh)),
            dma((8, nh)),
            dma((6,)),
            dma((2,)),
            dma((2, 2, nz // 2)),
            dma((2, 2, nz // 2)),
            dma((2, nz)),
            dma((2, nz)),
            dma((4,)),
        ],
        compiler_params=pltpu.CompilerParams(collective_id=0, has_side_effects=True),
        name="gather",
    )(q, do, k, v, ck, cv)


def dot(a, b, dim_a, dim_b):
    return lax.dot_general(a, b, (((dim_a,), (dim_b,)), ((), ())), preferred_element_type=F32)


def attention_kernel(
    listed, live, q_ref, do_ref, kn_ref, vn_ref, kv_ref,
    o_ref, dq_ref, dk_own, dv_own, dk_other, dv_other, dkv_ref,
    keys, values, bias, qs, dos, weights, dscores, acc,
):
    span = kn_ref.shape[0]
    rows = span // 2
    stores = kv_ref.shape[0]
    heads = q_ref.shape[1] // HEAD_SIZE
    keys[0:span] = kn_ref[...]
    values[0:span] = vn_ref[...]

    def fetch(s, carry):
        b = jnp.maximum(listed[s], 0)
        at = pl.ds(pl.multiple_of(span + s * BLK, BLK), BLK)
        keys[at] = kv_ref[s, 0, b]
        values[at] = kv_ref[s, 1, b]
        return carry

    lax.fori_loop(0, stores, fetch, 0, unroll=4)
    width = stores * BLK
    spread = lax.broadcasted_iota(jnp.int32, (stores, width), 1) // BLK == lax.broadcasted_iota(
        jnp.int32, (stores, width), 0
    )
    dead = (live[...] < 0).astype(F32)
    bias[:, 0:span] = jnp.zeros((1, span), F32)
    bias[:, span:] = dot(dead, spread.astype(F32), 1, 0) * -1e30

    def head(r, carry):
        col = lanes(r, HEAD_SIZE)
        q, do = q_ref[:, col], do_ref[:, col]
        t = dot(q, keys[...], 1, 1) * (SCALE * LOG2E) + bias[...]
        e = jnp.exp2(t - jnp.max(t, -1, keepdims=True))
        p = e * (1.0 / jnp.sum(e, -1, keepdims=True))
        w = p.astype(BF16)
        o = dot(w, values[...], 1, 0).astype(BF16)
        o_ref[:, col] = o
        row_dot = jnp.sum(do.astype(F32) * o.astype(F32), -1, keepdims=True)
        ds = (p * (dot(do, values[...], 1, 1) - row_dot)).astype(BF16)
        dq_ref[:, col] = (dot(ds, keys[...], 1, 0) * SCALE).astype(BF16)
        at = pl.ds(pl.multiple_of(r * rows, rows), rows)
        qs[at], dos[at], weights[at], dscores[at] = q, do, w, ds
        return carry

    lax.fori_loop(0, heads, head, 0)

    def emit(left, right, scale, own, other, i):
        g = dot(right[...], left[...], 0, 0).T
        if scale is not None:
            g = g * scale
        own[...] = g[0:rows]
        other[...] = g[rows:span].astype(BF16)
        acc[...] = g[span:].reshape(stores, BLK, HEAD_SIZE)

        def put(s, carry):
            value, b = acc[s], listed[s]
            for block in (0, 1):
                dkv_ref[s, i, block] = jnp.where(b == block, value, 0.0).astype(BF16)
            return carry

        lax.fori_loop(0, stores, put, 0, unroll=4)

    emit(dscores, qs, SCALE, dk_own, dk_other, 0)
    emit(weights, dos, None, dv_own, dv_other, 1)


def attention(listed, live, q, do, kn, vn, kv):
    rows, span, stores = q.shape[0], kn.shape[0], kv.shape[0]
    count = span + stores * BLK
    stacked = rows * (q.shape[1] // HEAD_SIZE)
    half = (span // 2, HEAD_SIZE)
    return pl.pallas_call(
        attention_kernel,
        out_shape=(
            jax.ShapeDtypeStruct(q.shape, BF16),
            jax.ShapeDtypeStruct(q.shape, BF16),
            jax.ShapeDtypeStruct(half, F32),
            jax.ShapeDtypeStruct(half, F32),
            jax.ShapeDtypeStruct(half, BF16),
            jax.ShapeDtypeStruct(half, BF16),
            jax.ShapeDtypeStruct(kv.shape, BF16),
        ),
        in_specs=[SMEM] + [VMEM] * 6,
        out_specs=(VMEM,) * 7,
        scratch_shapes=[
            pltpu.VMEM((count, HEAD_SIZE), BF16),
            pltpu.VMEM((count, HEAD_SIZE), BF16),
            pltpu.VMEM((1, count), F32),
            pltpu.VMEM((stacked, HEAD_SIZE), BF16),
            pltpu.VMEM((stacked, HEAD_SIZE), BF16),
            pltpu.VMEM((stacked, count), BF16),
            pltpu.VMEM((stacked, count), BF16),
            pltpu.VMEM((stores, BLK, HEAD_SIZE), F32),
        ],
        compiler_params=pltpu.CompilerParams(vmem_limit_bytes=60 * 2**20),
        name="attention",
    )(listed, live, q, do, kn, vn, kv)


def return_kernel(
    nz, nh, o, dq, dk_own, dv_own, dk_other, dv_other, dkv,
    o_out, dq_out, dk_out, dv_out, dck_out, dcv_out,
    from_x, ring_in, ring_out, opp_out, opp_in, pair_in, noisy, final, own_o, own_dq,
    out_send, out_recv, own_sem, pair_send, pair_recv, x_send, x_recv, z_send, z_recv, opp_sem,
):
    me = Place(nz, nh)
    mine = me.head
    qw, kw = o.shape[2], noisy.shape[3]
    greet(
        [me.head_peer(d) for d in range(1, nh)]
        + [me.partner(mine), me.z_peer(1), me.z_peer(-1), me.x_peer(1), me.x_peer(-1), me.x_peer(2)]
    )
    sends, heads = [], []

    def go(copy):
        copy.start()
        sends.append(copy)
        return copy

    order = [me.right]
    for far in range(me.right - 1, 0, -1):
        order += [far, -far]
    if me.left == me.right:
        order.insert(1, -me.right)
    order.append(0)
    sideways = {}
    for slot, far in enumerate(order):
        z = me.wrap_z(far)
        for i, d in enumerate((1, -1)):
            x = me.wrap_x(d)
            sideways[far, i] = go(
                remote(dkv.at[x, z], from_x.at[i, slot], x_send.at[i, slot], x_recv.at[i, slot], me.x_peer(d))
            )
    pair = [
        go(remote(src, pair_in.at[i], pair_send.at[i], pair_recv.at[i], me.partner(mine)))
        for i, src in enumerate((dk_other, dv_other))
    ]
    local = [
        pltpu.make_async_copy(o.at[mine], own_o, own_sem.at[0]),
        pltpu.make_async_copy(dq.at[mine], own_dq, own_sem.at[1]),
    ]
    for copy in local:
        copy.start()
    for i, (src, dst) in enumerate(((o, o_out), (dq, dq_out))):
        for d in range(1, nh):
            heads.append(
                go(
                    remote(
                        src.at[me.wrap_head(d)], dst.at[:, lanes(mine, qw)],
                        out_send.at[i, d], out_recv.at[i, d], me.head_peer(d),
                    )
                )
            )

    opposite = me.wrap_x(2)

    def term(unit, far):
        z = me.wrap_z(far)
        if unit == 1:
            return dkv[opposite, z].astype(F32)
        slot = order.index(far)
        for i in (0, 1):
            sideways[far, i].wait_recv()
        return dkv[me.x, z].astype(F32) + from_x[0, slot].astype(F32) + from_x[1, slot].astype(F32)

    steps = (me.right, me.left)
    flying = {}

    def noisy_sums():
        for i, own in enumerate((dk_own, dv_own)):
            pair[i].wait_recv()
            noisy[i] = (own[...] + pair_in[i].astype(F32)).astype(BF16)

    def noisy_out():
        for i, dst in enumerate((dk_out, dv_out)):
            for d in range(1, nh):
                heads.append(
                    go(
                        remote(
                            noisy.at[i, me.wrap_head(d)], dst.at[:, lanes(mine, kw)],
                            out_send.at[2 + i, d], out_recv.at[2 + i, d], me.head_peer(d),
                        )
                    )
                )

    for step in range(me.right):
        for unit in (1, 0):
            for direction in (0, 1):
                if step >= steps[direction]:
                    continue
                far = (steps[direction] - step) * (1 if direction == 0 else -1)
                total = term(unit, far)
                if step:
                    flying[direction, unit].wait_recv()
                    total = total + ring_in[direction, unit, step - 1].astype(F32)
                ring_out[direction, unit, step] = total.astype(BF16)
            for direction in (0, 1):
                if step >= steps[direction]:
                    continue
                flying[direction, unit] = go(
                    remote(
                        ring_out.at[direction, unit, step], ring_in.at[direction, unit, step],
                        z_send.at[direction, unit, step], z_recv.at[direction, unit, step],
                        me.z_peer(1 if direction == 0 else -1),
                    )
                )
        if step == 0:
            for copy in local:
                copy.wait()
            local = [
                pltpu.make_async_copy(own_o, o_out.at[:, lanes(mine, qw)], own_sem.at[0]),
                pltpu.make_async_copy(own_dq, dq_out.at[:, lanes(mine, qw)], own_sem.at[1]),
            ]
            for copy in local:
                copy.start()
            noisy_sums()
        if step == min(1, me.right - 1):
            noisy_out()
            for i, dst in enumerate((dk_out, dv_out)):
                local.append(
                    pltpu.make_async_copy(noisy.at[i, mine], dst.at[:, lanes(mine, kw)], own_sem.at[2 + i])
                )
                local[-1].start()

    def arrived(unit):
        total = term(unit, 0)
        for direction in (0, 1):
            if steps[direction]:
                flying[direction, unit].wait_recv()
                total = total + ring_in[direction, unit, steps[direction] - 1].astype(F32)
        return total

    opp_out[...] = arrived(1).astype(BF16)
    own_total = arrived(0)
    across = go(remote(opp_out, opp_in, opp_sem.at[0], opp_sem.at[1], me.x_peer(2)))
    across.wait_recv()
    final[...] = (own_total + opp_in[...].astype(F32)).astype(BF16)
    for d in range(1, nh):
        for i, dst in enumerate((dck_out, dcv_out)):
            heads.append(
                go(
                    remote(
                        final.at[i, me.wrap_head(d)], dst.at[:, lanes(mine, kw)],
                        out_send.at[4 + i, d], out_recv.at[4 + i, d], me.head_peer(d),
                    )
                )
            )
    for i, dst in enumerate((dck_out, dcv_out)):
        local.append(pltpu.make_async_copy(final.at[i, mine], dst.at[:, lanes(mine, kw)], own_sem.at[4 + i]))
        local[-1].start()
    for copy in heads:
        copy.wait_recv()
    for copy in sends:
        copy.wait_send()
    for copy in local:
        copy.wait()


def give_back(nz, nh, o, dq, dk_own, dv_own, dk_other, dv_other, dkv):
    rows, qw, kw, crows = o.shape[1], o.shape[2], dk_own.shape[2], dkv.shape[4]
    dma = pltpu.SemaphoreType.DMA
    wide = jax.ShapeDtypeStruct((rows, nh * qw), BF16)
    narrow = jax.ShapeDtypeStruct((rows, nh * kw), BF16)
    clean = jax.ShapeDtypeStruct((crows, nh * kw), BF16)
    half = nz // 2
    unit = (2, nh, crows, kw)
    return pl.pallas_call(
        functools.partial(return_kernel, nz, nh),
        out_shape=(wide, wide, narrow, narrow, clean, clean),
        in_specs=[ANY, ANY] + [VMEM] * 5,
        out_specs=(ANY,) * 6,
        scratch_shapes=[
            pltpu.VMEM((2, nz) + unit, BF16),
            pltpu.VMEM((2, 2, half) + unit, BF16),
            pltpu.VMEM((2, 2, half) + unit, BF16),
            pltpu.VMEM(unit, BF16),
            pltpu.VMEM(unit, BF16),
            pltpu.VMEM((2, nh, rows, kw), BF16),
            pltpu.VMEM((2, nh, rows, kw), BF16),
            pltpu.VMEM(unit, BF16),
            pltpu.VMEM((rows, qw), BF16),
            pltpu.VMEM((rows, qw), BF16),
            dma((6, nh)),
            dma((6, nh)),
            dma((6,)),
            dma((2,)),
            dma((2,)),
            dma((2, nz)),
            dma((2, nz)),
            dma((2, 2, half)),
            dma((2, 2, half)),
            dma((2,)),
        ],
        compiler_params=pltpu.CompilerParams(collective_id=1, has_side_effects=True),
        name="give_back",
    )(o, dq, dk_own, dv_own, dk_other, dv_other, dkv)


def shards(nz, nh, queries, nk, nv, ck, cv, output_gradient, history_list):
    qg, dog, kn, vn, kv = gather(nz, nh, queries, output_gradient, nk, nv, ck, cv)
    rows = nh * queries.shape[0]
    stores = NX * nz
    listed = lax.dynamic_index_in_dim(history_list, lax.axis_index("ctx"), 0, keepdims=False)
    o, dq, dk_own, dv_own, dk_other, dv_other, dkv = attention(
        listed,
        listed[None],
        qg.reshape(rows, -1),
        dog.reshape(rows, -1),
        kn.reshape(2 * rows, HEAD_SIZE),
        vn.reshape(2 * rows, HEAD_SIZE),
        kv.reshape(stores, 2, -1, BLK, HEAD_SIZE),
    )
    noisy = (nh, queries.shape[0], HEAD_SIZE)
    return give_back(
        nz,
        nh,
        o.reshape(qg.shape),
        dq.reshape(qg.shape),
        dk_own.reshape(noisy),
        dv_own.reshape(noisy),
        dk_other.reshape(noisy),
        dv_other.reshape(noisy),
        dkv.reshape(kv.shape),
    )


def solution(mesh):
    nz, nh = mesh.shape["ctx"] // NX, mesh.shape["head"]
    tokens = P(("ctx", "head"), None)
    return jax.shard_map(
        functools.partial(shards, nz, nh),
        mesh=mesh,
        in_specs=(tokens,) * 6 + (P(),),
        out_specs=(tokens,) * 6,
        check_vma=False,
    )
```

```python
import functools

import jax
import jax.numpy as jnp
from jax import lax
from jax.experimental import pallas as pl
from jax.experimental.pallas import tpu as pltpu
from jax.sharding import PartitionSpec as P

BLK = 32
HEAD_SIZE = 128
SCALE = HEAD_SIZE**-0.5
LOG2E = 1.4426950408889634
NX = 4
F32 = jnp.float32
BF16 = jnp.bfloat16
MESH = pl.DeviceIdType.MESH
ANY = pl.BlockSpec(memory_space=pl.ANY)
VMEM = pl.BlockSpec(memory_space=pltpu.VMEM)
SMEM = pl.BlockSpec(memory_space=pltpu.SMEM)


class Place:
    def __init__(self, nz, nh):
        self.nz, self.nh = nz, nh
        ctx = lax.axis_index("ctx")
        self.head = lax.axis_index("head")
        self.x = ctx // nz
        self.z = ctx % nz
        self.right = nz // 2
        self.left = nz - 1 - nz // 2

    def wrap_x(self, d):
        return lax.rem(self.x + (d + NX), NX)

    def wrap_z(self, d):
        return lax.rem(self.z + (d + self.nz), self.nz)

    def wrap_head(self, d):
        return lax.rem(self.head + (d + self.nh), self.nh)

    def at(self, x, z, head):
        return (x * self.nz + z, head)

    def x_peer(self, d):
        return self.at(self.wrap_x(d), self.z, self.head)

    def z_peer(self, d):
        return self.at(self.x, self.wrap_z(d), self.head)

    def head_peer(self, d):
        return self.at(self.x, self.z, self.wrap_head(d))

    def z_peers(self):
        return [self.z_peer(d) for d in (1, -1) + ((2, -2) if self.right > 1 else ())]

    def partner_z(self):
        return self.z + 1 - 2 * lax.rem(self.z, 2)

    def partner(self, head):
        return self.at(self.x, self.partner_z(), head)


def greet(peers):
    barrier = pltpu.get_barrier_semaphore()
    for peer in peers:
        pl.semaphore_signal(barrier, inc=1, device_id=peer, device_id_type=MESH)
    pl.semaphore_wait(barrier, len(peers))


def remote(src, dst, send, recv, peer):
    return pltpu.make_async_remote_copy(
        src_ref=src, dst_ref=dst, send_sem=send, recv_sem=recv, device_id=peer, device_id_type=MESH
    )


def lanes(index, width):
    return pl.ds(pl.multiple_of(index * width, 128), width)


def dot(a, b, dim_a, dim_b):
    return lax.dot_general(a, b, (((dim_a,), (dim_b,)), ((), ())), preferred_element_type=F32)


SIDES = (0, 1, -1, 2)
OWN, RIGHT, LEFT, FAR = range(4)


def kernel(
    nz, nh, listed, q, do, k, v, ck, cv,
    o_out, dq_out, dk_out, dv_out, dck_out, dcv_out, qg, dog, kn, vn, og, dqg, ng,
    kv, own_q, own_do, own_k, own_v, q_all, do_all, o_all, dq_all, qs, dos, keys, values,
    t, dp, peak, weights, dscores, bias, terms, relay_in, relay_out, from_x, ring_in, ring_out,
    other, pair_in, span_grad, noisy_sum, final,
    in_send, in_recv, own_sem, load_sem, gz_send, gz_recv, gx_send, gx_recv,
    out_send, out_recv, put_sem, pair_send, pair_recv, x_send, x_recv, z_send, z_recv,
):
    me = Place(nz, nh)
    mine = me.head
    qw, kw = q.shape[1] // nh, k.shape[1] // nh
    few = q.shape[0]
    rows = few * nh
    span = 2 * rows
    heads = qw // HEAD_SIZE
    half = nz // 2
    width = half * BLK
    reach = (me.right, me.left)
    offsets = [0] + [d * sign for d in range(1, half) for sign in (1, -1)] + [half]
    slot_of = {off: p for p, off in enumerate(offsets)}
    slot_of[-half] = slot_of[half]

    sends = []

    def go(copy):
        copy.start()
        sends.append(copy)
        return copy

    def token_rows(index):
        return pl.ds(pl.multiple_of(index * few, 8), few)

    local = [
        pltpu.make_async_copy(ck.at[:, lanes(mine, kw)], kv.at[OWN, 0, 0, mine], own_sem.at[0]),
        pltpu.make_async_copy(cv.at[:, lanes(mine, kw)], kv.at[OWN, 0, 1, mine], own_sem.at[1]),
        pltpu.make_async_copy(k.at[:, lanes(mine, kw)], own_k, own_sem.at[2]),
        pltpu.make_async_copy(v.at[:, lanes(mine, kw)], own_v, own_sem.at[3]),
        pltpu.make_async_copy(q.at[:, lanes(mine, qw)], own_q, own_sem.at[4]),
        pltpu.make_async_copy(do.at[:, lanes(mine, qw)], own_do, own_sem.at[5]),
    ]
    for copy in local:
        copy.start()
    greet([me.head_peer(d) for d in range(1, nh)] + me.z_peers() + [me.x_peer(1), me.x_peer(-1)])

    def spread(which, src, dst_at, size):
        copies = []
        for d in range(1, nh):
            copies.append(
                go(
                    remote(
                        src.at[:, lanes(me.wrap_head(d), size)], dst_at(mine),
                        in_send.at[which, d], in_recv.at[which, d], me.head_peer(d),
                    )
                )
            )
        return copies

    clean = [spread(i, src, lambda j, i=i: kv.at[OWN, 0, i, j], kw) for i, src in enumerate((ck, cv))]
    noisy = [spread(2 + i, src, lambda j, dst=dst: dst.at[token_rows(j)], kw) for i, (src, dst) in enumerate(((k, kn), (v, vn)))]
    wide = [spread(4 + i, src, lambda j, dst=dst: dst.at[token_rows(j)], qw) for i, (src, dst) in enumerate(((q, qg), (do, dog)))]
    for copy in local[:2] :
        copy.wait()
    for copy in sum(clean, []):
        copy.wait_recv()

    arriving, sideways, across = {}, {}, {}

    def source(direction, far):
        return slot_of[-far if direction == 0 else far]

    def hop(direction, far, stride):
        arriving[direction, far + stride] = go(
            remote(
                kv.at[OWN, source(direction, far)], kv.at[OWN, source(direction, far + stride)],
                gz_send.at[direction, far + stride], gz_recv.at[direction, far + stride],
                me.z_peer(stride if direction == 0 else -stride),
            )
        )

    def pass_on(p):
        for i, (d, side) in enumerate(((1, LEFT), (-1, RIGHT))):
            sideways[p, i] = go(
                remote(kv.at[OWN, p], kv.at[side, p], gx_send.at[i, p], gx_recv.at[i, p], me.x_peer(d))
            )

    def hand_over(p):
        for i in (0, 1):
            sideways[p, i].wait_recv()
        side, d = (RIGHT, -1) if p % 2 else (LEFT, 1)
        across[p] = go(remote(kv.at[side, p], kv.at[FAR, p], gx_send.at[2, p], gx_recv.at[2, p], me.x_peer(d)))

    def block_of(side, p):
        return listed[me.wrap_x(SIDES[side]) * nz + me.wrap_z(offsets[p])]

    def column(side, part):
        return span + side * nz * BLK + part * width

    def score(low, count):
        kk, vv = keys[low : low + count], values[low : low + count]

        def body(r, carry):
            at = pl.ds(pl.multiple_of(r * rows, rows), rows)
            s = dot(qs[at], kk, 1, 1) * (SCALE * LOG2E) + bias[:, low : low + count]
            t[at, low : low + count] = s
            dp[at, low : low + count] = dot(dos[at], vv, 1, 1)
            top = peak[at]
            if count % HEAD_SIZE:
                top = jnp.maximum(top, jnp.max(s, -1, keepdims=True))
            else:
                for j in range(0, count, HEAD_SIZE):
                    top = jnp.maximum(top, s[:, j : j + HEAD_SIZE])
            peak[at] = top
            return carry

        lax.fori_loop(0, heads, body, 0)

    def score_clean(side, part):
        low = column(side, part)
        place = lax.broadcasted_iota(jnp.int32, (1, width), 1) // BLK
        dead = jnp.zeros((1, width), F32)
        for j in range(half):
            p = part * half + j
            b = block_of(side, p)
            for i, dst in enumerate((keys, values)):
                both = kv[side, p, i].astype(F32).reshape(2 * BLK, kw)
                dst[low + j * BLK : low + (j + 1) * BLK] = jnp.where(b == 1, both[BLK:], both[:BLK]).astype(BF16)
            dead = jnp.where(place == j, jnp.where(b < 0, -1e30, 0.0), dead)
        bias[:, low : low + width] = dead
        score(low, width)

    def score_noisy():
        for copy in back + loads:
            copy.wait()
        for copy in pair_kv:
            copy.wait_recv()
        pulls = [pltpu.make_async_copy(src, dst.at[0:span], load_sem.at[2 + i]) for i, (src, dst) in enumerate(((kn, keys), (vn, values)))]
        for copy in pulls:
            copy.start()
        for r in range(heads):
            at, col = slice(r * rows, (r + 1) * rows), slice(r * HEAD_SIZE, (r + 1) * HEAD_SIZE)
            qs[at] = q_all[:, col]
            dos[at] = do_all[:, col]
        bias[:, 0:span] = jnp.zeros((1, span), F32)
        peak[...] = jnp.full(peak.shape, -3e38, F32)
        for copy in pulls:
            copy.wait()
        score(0, span)

    rounds = [[(0, 0)]]
    for near in range(1, me.right + 1, 2):
        rounds.append([(w, far) for far in (near, near + 1) for w in (0, 1) if far <= reach[w]])

    def advance(r):
        for direction, far in rounds[r]:
            if r == 0:
                for stride in (1, 2):
                    for w in (0, 1):
                        if stride <= reach[w]:
                            hop(w, 0, stride)
            else:
                arriving[direction, far].wait_recv()
                if far + 2 <= reach[direction]:
                    hop(direction, far, 2)
            pass_on(source(direction, far))

    def hand_round(r):
        for unit in rounds[r]:
            hand_over(source(*unit))

    last = len(rounds) - 1
    for r in range(last + 1):
        advance(r)
        if r == min(1, last):
            for copy in local[2:]:
                copy.wait()
            back = [
                pltpu.make_async_copy(src, dst.at[token_rows(mine)], own_sem.at[i])
                for i, (src, dst) in enumerate(((own_k, kn), (own_v, vn), (own_q, qg), (own_do, dog)))
            ]
            for copy in back:
                copy.start()
        if r == min(2, last):
            for copy in sum(noisy, []):
                copy.wait_recv()
            for copy in back:
                copy.wait()
            back = []
            pair_kv = [
                go(
                    remote(
                        ref.at[0:rows], ref.at[rows:span], in_send.at[6 + i, 0], in_recv.at[6 + i, 0],
                        me.partner(mine),
                    )
                )
                for i, ref in enumerate((kn, vn))
            ]
            for copy in sum(wide, []):
                copy.wait_recv()
            loads = [pltpu.make_async_copy(src, dst, load_sem.at[i]) for i, (src, dst) in enumerate(((qg, q_all), (dog, do_all)))]
            for copy in loads:
                copy.start()
        if r >= 2:
            hand_round(r - 2)
        if r == max(last - 1, min(2, last)):
            score_noisy()
            if last > 2:
                score_clean(OWN, 0)
    if last <= 2:
        score_clean(OWN, 0)
    if last > 0:
        hand_round(last - 1)
    score_clean(OWN, 1)
    done = sum(len(units) for units in rounds[:last])
    early = done >= half
    if early:
        score_clean(RIGHT, 0)
        score_clean(LEFT, 0)
    hand_round(last)
    if not early:
        score_clean(RIGHT, 0)
        score_clean(LEFT, 0)
    score_clean(RIGHT, 1)
    score_clean(LEFT, 1)
    for part in (0, 1):
        for p in range(part * half, (part + 1) * half):
            across[p].wait_recv()
        score_clean(FAR, part)

    def finish(r, carry):
        at = pl.ds(pl.multiple_of(r * rows, rows), rows)
        col = lanes(r, HEAD_SIZE)
        e = jnp.exp2(t[at] - jnp.max(peak[at], -1, keepdims=True))
        prob = e * (1.0 / jnp.sum(e, -1, keepdims=True))
        w = prob.astype(BF16)
        weights[at] = w
        o = dot(w, values[...], 1, 0).astype(BF16)
        o_all[:, col] = o
        row_dot = jnp.sum(dos[at].astype(F32) * o.astype(F32), -1, keepdims=True)
        ds = (prob * (dp[at] - row_dot)).astype(BF16)
        dscores[at] = ds
        dq_all[:, col] = (dot(ds, keys[...], 1, 0) * SCALE).astype(BF16)
        return carry

    lax.fori_loop(0, heads, finish, 0)
    puts = [pltpu.make_async_copy(src, dst, put_sem.at[i]) for i, (src, dst) in enumerate(((o_all, og), (dq_all, dqg)))]
    for copy in puts:
        copy.start()

    def gradients(low, count):
        at = slice(low, low + count)
        return dot(qs[...], dscores[:, at], 0, 0).T * SCALE, dot(dos[...], weights[:, at], 0, 0).T

    def make_terms(side, part):
        for i, g in enumerate(gradients(column(side, part), width)):
            for j in range(half):
                p = part * half + j
                b = block_of(side, p)
                value = g[j * BLK : (j + 1) * BLK]
                both = [jnp.where(b == block, value, 0.0) for block in (0, 1)]
                terms[side, p, i] = jnp.concatenate(both, 0).reshape(terms.shape[3:]).astype(BF16)

    rounds = []
    for step in range((me.right + 1) // 2):
        rounds.append([(w, reach[w] - 2 * step - i) for i in (0, 1) for w in (0, 1) if reach[w] - 2 * step - i > 0])
    rounds.append([(0, 0)])
    first, direct, second, flying = {}, {}, {}, {}

    def target(direction, far):
        return slot_of[far if direction == 0 else -far]

    def slots(r):
        return [target(*unit) for unit in rounds[r]] if r < len(rounds) else []

    def send_first(r):
        for p in slots(r):
            first[p] = go(
                remote(terms.at[FAR, p], relay_in.at[p], x_send.at[0, p], x_recv.at[0, p], me.x_peer(-1 if p % 2 else 1))
            )

    def send_direct(r):
        for p in slots(r):
            side, d = (RIGHT, 1) if p % 2 else (LEFT, -1)
            direct[p] = go(
                remote(terms.at[side, p], from_x.at[0, p], x_send.at[1, p], x_recv.at[1, p], me.x_peer(d))
            )

    def send_second(r):
        for p in slots(r):
            first[p].wait_recv()
            side = LEFT if p % 2 else RIGHT
            relay_out[p] = (relay_in[p].astype(F32) + terms[side, p].astype(F32)).astype(BF16)
        for p in slots(r):
            second[p] = go(
                remote(relay_out.at[p], from_x.at[1, p], x_send.at[2, p], x_recv.at[2, p], me.x_peer(-1 if p % 2 else 1))
            )

    def total(direction, far):
        p = target(direction, far)
        direct[p].wait_recv()
        second[p].wait_recv()
        value = terms[OWN, p].astype(F32) + from_x[0, p].astype(F32) + from_x[1, p].astype(F32)
        before = [(direction, far + 2)] if far else [(w, f) for f in (1, 2) for w in (0, 1)]
        for w, f in before:
            if f <= reach[w]:
                flying[w, f].wait_recv()
                value = value + ring_in[w, f].astype(F32)
        return value.astype(BF16)

    def send_ring(r):
        for direction, far in rounds[r]:
            ring_out[direction, far] = total(direction, far)
        for direction, far in rounds[r]:
            stride = min(2, far)
            flying[direction, far] = go(
                remote(
                    ring_out.at[direction, far], ring_in.at[direction, far],
                    z_send.at[direction, far], z_recv.at[direction, far],
                    me.z_peer(stride if direction == 0 else -stride),
                )
            )

    def head_out(which, src_at, dst, size):
        copies = []
        for d in range(1, nh):
            copies.append(
                go(
                    remote(
                        src_at(me.wrap_head(d)), dst.at[:, lanes(mine, size)],
                        out_send.at[which, d], out_recv.at[which, d], me.head_peer(d),
                    )
                )
            )
        return copies

    results = []
    make_terms(FAR, 1)
    send_first(0)
    send_first(1)
    make_terms(RIGHT, 1)
    make_terms(LEFT, 1)
    send_direct(0)
    make_terms(OWN, 1)
    for copy in puts:
        copy.wait()
    mids = [
        pltpu.make_async_copy(og.at[token_rows(mine)], own_q, own_sem.at[0]),
        pltpu.make_async_copy(dqg.at[token_rows(mine)], own_do, own_sem.at[1]),
    ]
    for copy in mids:
        copy.start()
    for i, (src, dst) in enumerate(((og, o_out), (dqg, dq_out))):
        results += head_out(i, lambda j, src=src: src.at[token_rows(j)], dst, qw)
    for i, g in enumerate(gradients(0, span)):
        span_grad[i] = g[0:rows]
        other[i] = g[rows:span].astype(BF16)
    send_second(0)
    send_direct(1)
    pair = [
        go(remote(other.at[i], pair_in.at[i], pair_send.at[i], pair_recv.at[i], me.partner(mine))) for i in (0, 1)
    ]
    make_terms(FAR, 0)
    send_first(2)
    make_terms(RIGHT, 0)
    make_terms(LEFT, 0)
    send_second(1)
    send_direct(2)
    send_first(3)
    send_ring(0)
    make_terms(OWN, 0)
    for copy in mids:
        copy.wait()
    mids = [
        pltpu.make_async_copy(own_q, o_out.at[:, lanes(mine, qw)], own_sem.at[0]),
        pltpu.make_async_copy(own_do, dq_out.at[:, lanes(mine, qw)], own_sem.at[1]),
    ]
    for copy in mids:
        copy.start()
    for i in (0, 1):
        pair[i].wait_recv()
        noisy_sum[i] = (span_grad[i] + pair_in[i].astype(F32)).astype(BF16)
    put = pltpu.make_async_copy(noisy_sum, ng, put_sem.at[0])
    put.start()
    for r in range(1, len(rounds)):
        if r > 1:
            send_direct(r + 1)
            send_first(r + 2)
        if r + 1 < len(rounds) or r == 1:
            send_second(r + 1)
        if r == len(rounds) - 1:
            break
        send_ring(r)
        if r == 1:
            put.wait()
            tail = [pltpu.make_async_copy(ng.at[i, token_rows(mine)], ref, own_sem.at[2 + i]) for i, ref in enumerate((own_k, own_v))]
            for copy in tail:
                copy.start()
            for i, dst in enumerate((dk_out, dv_out)):
                results += head_out(2 + i, lambda j, i=i: ng.at[i, token_rows(j)], dst, kw)
            for copy in tail:
                copy.wait()
            for i, (ref, dst) in enumerate(((own_k, dk_out), (own_v, dv_out))):
                mids.append(pltpu.make_async_copy(ref, dst.at[:, lanes(mine, kw)], own_sem.at[2 + i]))
                mids[-1].start()
    final[...] = total(0, 0)
    for i, dst in enumerate((dck_out, dcv_out)):
        results += head_out(4 + i, lambda j, i=i: final.at[i, j], dst, kw)
        mids.append(pltpu.make_async_copy(final.at[i, mine], dst.at[:, lanes(mine, kw)], own_sem.at[4 + i]))
        mids[-1].start()
    for copy in results:
        copy.wait_recv()
    for copy in sends:
        copy.wait_send()
    for copy in mids:
        copy.wait()


def everything(nz, nh, listed, q, do, k, v, ck, cv):
    few, qw, kw, crows = q.shape[0], q.shape[1] // nh, k.shape[1] // nh, ck.shape[0]
    rows = few * nh
    span = 2 * rows
    count = span + NX * nz * BLK
    stacked = rows * (qw // HEAD_SIZE)
    half = nz // 2
    unit = (2, nh, crows, kw)
    dma = pltpu.SemaphoreType.DMA

    def shape(*dims):
        return jax.ShapeDtypeStruct(dims, BF16)

    return pl.pallas_call(
        functools.partial(kernel, nz, nh),
        out_shape=(
            shape(few, nh * qw), shape(few, nh * qw), shape(few, nh * kw), shape(few, nh * kw),
            shape(crows, nh * kw), shape(crows, nh * kw),
            shape(rows, qw), shape(rows, qw), shape(span, kw), shape(span, kw),
            shape(rows, qw), shape(rows, qw), shape(2, rows, kw),
        ),
        in_specs=[SMEM] + [ANY] * 6,
        out_specs=(ANY,) * 13,
        scratch_shapes=[
            pltpu.VMEM((NX, nz) + unit, BF16),
            pltpu.VMEM((few, qw), BF16),
            pltpu.VMEM((few, qw), BF16),
            pltpu.VMEM((few, kw), BF16),
            pltpu.VMEM((few, kw), BF16),
            pltpu.VMEM((rows, qw), BF16),
            pltpu.VMEM((rows, qw), BF16),
            pltpu.VMEM((rows, qw), BF16),
            pltpu.VMEM((rows, qw), BF16),
            pltpu.VMEM((stacked, kw), BF16),
            pltpu.VMEM((stacked, kw), BF16),
            pltpu.VMEM((count, kw), BF16),
            pltpu.VMEM((count, kw), BF16),
            pltpu.VMEM((stacked, count), F32),
            pltpu.VMEM((stacked, count), F32),
            pltpu.VMEM((stacked, HEAD_SIZE), F32),
            pltpu.VMEM((stacked, count), BF16),
            pltpu.VMEM((stacked, count), BF16),
            pltpu.VMEM((1, count), F32),
            pltpu.VMEM((NX, nz) + unit, BF16),
            pltpu.VMEM((nz,) + unit, BF16),
            pltpu.VMEM((nz,) + unit, BF16),
            pltpu.VMEM((2, nz) + unit, BF16),
            pltpu.VMEM((2, half + 1) + unit, BF16),
            pltpu.VMEM((2, half + 1) + unit, BF16),
            pltpu.VMEM((2, rows, kw), BF16),
            pltpu.VMEM((2, rows, kw), BF16),
            pltpu.VMEM((2, rows, kw), F32),
            pltpu.VMEM((2, rows, kw), BF16),
            pltpu.VMEM(unit, BF16),
            dma((8, nh)), dma((8, nh)), dma((6,)), dma((4,)),
            dma((2, half + 1)), dma((2, half + 1)), dma((3, nz)), dma((3, nz)),
            dma((6, nh)), dma((6, nh)), dma((2,)), dma((2,)), dma((2,)),
            dma((3, nz)), dma((3, nz)), dma((2, half + 1)), dma((2, half + 1)),
        ],
        compiler_params=pltpu.CompilerParams(
            collective_id=0, has_side_effects=True, vmem_limit_bytes=60 * 2**20
        ),
        name="everything",
    )(listed, q, do, k, v, ck, cv)


def settle_kernel(*refs):
    count = len(refs) // 3
    ins, outs, held = refs[:count], refs[count : 2 * count], refs[2 * count : 3 * count]
    sem = refs[3 * count]
    loads = [pltpu.make_async_copy(a, b, sem.at[0, i]) for i, (a, b) in enumerate(zip(ins, held))]
    stores = [pltpu.make_async_copy(a, b, sem.at[1, i]) for i, (a, b) in enumerate(zip(held, outs))]
    for copy in loads:
        copy.start()
    for load, store in zip(loads, stores):
        load.wait()
        store.start()
    for copy in stores:
        copy.wait()


def settle(arrays):
    shapes = [(a.shape, a.dtype) for a in arrays]
    return pl.pallas_call(
        settle_kernel,
        out_shape=tuple(jax.ShapeDtypeStruct(*s) for s in shapes),
        in_specs=[ANY] * len(arrays),
        out_specs=(ANY,) * len(arrays),
        scratch_shapes=[pltpu.VMEM(*s) for s in shapes]
        + [pltpu.SemaphoreType.DMA((2, len(arrays)))] ,
        name="settle",
    )(*arrays)


def shards(nz, nh, queries, nk, nv, ck, cv, output_gradient, history_list):
    listed = lax.dynamic_index_in_dim(history_list, lax.axis_index("ctx"), 0, keepdims=False)
    results = everything(nz, nh, listed, queries, output_gradient, nk, nv, ck, cv)
    return settle(results[:6])


def solution(mesh):
    nz, nh = mesh.shape["ctx"] // NX, mesh.shape["head"]
    tokens = P(("ctx", "head"), None)
    return jax.shard_map(
        functools.partial(shards, nz, nh),
        mesh=mesh,
        in_specs=(tokens,) * 6 + (P(),),
        out_specs=(tokens,) * 6,
        check_vma=False,
    )
```

```python
import functools

import jax
import jax.numpy as jnp
from jax import lax
from jax.experimental import pallas as pl
from jax.experimental.pallas import tpu as pltpu
from jax.sharding import PartitionSpec as P

BLK = 32
HEAD_SIZE = 128
SCALE = HEAD_SIZE**-0.5
LOG2E = 1.4426950408889634
NX = 4
F32 = jnp.float32
BF16 = jnp.bfloat16
MESH = pl.DeviceIdType.MESH
ANY = pl.BlockSpec(memory_space=pl.ANY)
VMEM = pl.BlockSpec(memory_space=pltpu.VMEM)
SMEM = pl.BlockSpec(memory_space=pltpu.SMEM)


class Place:
    def __init__(self, nz, nh):
        self.nz, self.nh = nz, nh
        ctx = lax.axis_index("ctx")
        self.head = lax.axis_index("head")
        self.x = ctx // nz
        self.z = ctx % nz
        self.right = nz // 2
        self.left = nz - 1 - nz // 2

    def wrap_x(self, d):
        return lax.rem(self.x + (d + NX), NX)

    def wrap_z(self, d):
        return lax.rem(self.z + (d + self.nz), self.nz)

    def wrap_head(self, d):
        return lax.rem(self.head + (d + self.nh), self.nh)

    def at(self, x, z, head):
        return (x * self.nz + z, head)

    def x_peer(self, d):
        return self.at(self.wrap_x(d), self.z, self.head)

    def z_peer(self, d):
        return self.at(self.x, self.wrap_z(d), self.head)

    def head_peer(self, d):
        return self.at(self.x, self.z, self.wrap_head(d))

    def z_peers(self):
        return [self.z_peer(d) for d in (1, -1) + ((2, -2) if self.right > 1 else ())]

    def partner_z(self):
        return self.z + 1 - 2 * lax.rem(self.z, 2)

    def partner(self, head):
        return self.at(self.x, self.partner_z(), head)


def greet(peers):
    barrier = pltpu.get_barrier_semaphore()
    for peer in peers:
        pl.semaphore_signal(barrier, inc=1, device_id=peer, device_id_type=MESH)
    pl.semaphore_wait(barrier, len(peers))


def remote(src, dst, send, recv, peer):
    return pltpu.make_async_remote_copy(
        src_ref=src, dst_ref=dst, send_sem=send, recv_sem=recv, device_id=peer, device_id_type=MESH
    )


def lanes(index, width):
    return pl.ds(pl.multiple_of(index * width, 128), width)


def dot(a, b, dim_a, dim_b):
    return lax.dot_general(a, b, (((dim_a,), (dim_b,)), ((), ())), preferred_element_type=F32)


SIDES = (0, 1, -1, 2)
OWN, RIGHT, LEFT, FAR = range(4)


def kernel(
    nz, nh, history, q, do, k, v, ck, cv,
    o_out, dq_out, dk_out, dv_out, dck_out, dcv_out, qg, dog, kn, vn, og, dqg, ng, kp, vp,
    listed, kv, own_q, own_do, own_k, own_v, own_kp, own_vp, q_all, do_all, o_all, dq_all, qs, dos, keys, values,
    t, dp, tops, peak, norm, acc, weights, dscores, bias, terms, relay_in, relay_out, direct_in, second_in, ring_in, ring_out,
    other, pair_in, span_grad, noisy_sum, final,
    list_sem, in_send, in_recv, own_sem, load_sem, gz_send, gz_recv, gx_send, gx_recv,
    out_send, out_recv, put_sem, pair_send, pair_recv, x_send, x_recv, z_send, z_recv,
):
    me = Place(nz, nh)
    mine = me.head
    qw, kw = q.shape[1] // nh, k.shape[1] // nh
    few = q.shape[0]
    rows = few * nh
    span = 2 * rows
    heads = qw // HEAD_SIZE
    half = nz // 2
    width = half * BLK
    reach = (me.right, me.left)
    offsets = [0] + [d * sign for d in range(1, half) for sign in (1, -1)] + [half]
    slot_of = {off: p for p, off in enumerate(offsets)}
    slot_of[-half] = slot_of[half]

    sends = []

    def go(copy):
        copy.start()
        sends.append(copy)
        return copy

    def token_rows(index):
        return pl.ds(pl.multiple_of(index * few, 8), few)

    ctx = lax.axis_index("ctx")
    listing = pltpu.make_async_copy(history, listed, list_sem)
    listing.start()
    local = [
        pltpu.make_async_copy(ck.at[:, lanes(mine, kw)], kv.at[OWN, 0, 0, mine], own_sem.at[0]),
        pltpu.make_async_copy(cv.at[:, lanes(mine, kw)], kv.at[OWN, 0, 1, mine], own_sem.at[1]),
        pltpu.make_async_copy(k.at[:, lanes(mine, kw)], own_k, own_sem.at[2]),
        pltpu.make_async_copy(v.at[:, lanes(mine, kw)], own_v, own_sem.at[3]),
        pltpu.make_async_copy(q.at[:, lanes(mine, qw)], own_q, own_sem.at[4]),
        pltpu.make_async_copy(do.at[:, lanes(mine, qw)], own_do, own_sem.at[5]),
    ]
    for copy in local:
        copy.start()
    greet([me.head_peer(d) for d in range(1, nh)] + me.z_peers() + [me.x_peer(1), me.x_peer(-1)])

    def spread(which, src, dst_at, size):
        copies = []
        for d in range(1, nh):
            copies.append(
                go(
                    remote(
                        src.at[:, lanes(me.wrap_head(d), size)], dst_at(mine),
                        in_send.at[which, d], in_recv.at[which, d], me.head_peer(d),
                    )
                )
            )
        return copies

    clean = [spread(i, src, lambda j, i=i: kv.at[OWN, 0, i, j], kw) for i, src in enumerate((ck, cv))]
    noisy = [spread(2 + i, src, lambda j, dst=dst: dst.at[token_rows(j)], kw) for i, (src, dst) in enumerate(((k, kn), (v, vn)))]
    wide = [spread(4 + i, src, lambda j, dst=dst: dst.at[token_rows(j)], qw) for i, (src, dst) in enumerate(((q, qg), (do, dog)))]
    pair_kv = [
        go(remote(src, dst, in_send.at[6 + i, 0], in_recv.at[6 + i, 0], me.partner(mine)))
        for i, (src, dst) in enumerate(((k, kp), (v, vp)))
    ]
    for copy in local[:2]:
        copy.wait()
    for copy in sum(clean, []):
        copy.wait_recv()

    arriving, sideways, across = {}, {}, {}

    def source(direction, far):
        return slot_of[-far if direction == 0 else far]

    def hop(direction, far, stride, i):
        arriving[direction, far + stride, i] = go(
            remote(
                kv.at[OWN, source(direction, far), i], kv.at[OWN, source(direction, far + stride), i],
                gz_send.at[direction, far + stride, i], gz_recv.at[direction, far + stride, i],
                me.z_peer(stride if direction == 0 else -stride),
            )
        )

    def pass_on(p):
        for i, (d, side) in enumerate(((1, LEFT), (-1, RIGHT))):
            sideways[p, i] = go(
                remote(kv.at[OWN, p], kv.at[side, p], gx_send.at[i, p], gx_recv.at[i, p], me.x_peer(d))
            )

    def hand_over(p):
        for i in (0, 1):
            sideways[p, i].wait_recv()
        side, d = (RIGHT, -1) if p % 2 else (LEFT, 1)
        across[p] = go(remote(kv.at[side, p], kv.at[FAR, p], gx_send.at[2, p], gx_recv.at[2, p], me.x_peer(d)))

    def block_of(side, p):
        return listed[ctx, me.wrap_x(SIDES[side]) * nz + me.wrap_z(offsets[p])]

    def column(side, part):
        return span + side * nz * BLK + part * width

    chunks = [(0, span)] + [(column(side, part), width) for side in range(NX) for part in (0, 1)]

    def score(index):
        low, count = chunks[index]
        kk, vv = keys[low : low + count], values[low : low + count]
        for r in range(heads):
            at = slice(r * rows, (r + 1) * rows)
            s = dot(qs[at], kk, 1, 1) * (SCALE * LOG2E)
            if index:
                s = s + bias[:, low : low + count]
            groups = [s[:, j : j + HEAD_SIZE] for j in range(0, count, HEAD_SIZE)]
            most = jnp.max(functools.reduce(jnp.maximum, groups), -1, keepdims=True)
            if index:
                old = peak[at]
                top = jnp.maximum(old, most)
            else:
                top = jnp.broadcast_to(most, (rows, HEAD_SIZE))
            groups = [jnp.exp2(g - top) for g in groups]
            for j, g in enumerate(groups):
                t[at, low + j * HEAD_SIZE : low + (j + 1) * HEAD_SIZE] = g
            tops[index, at] = top
            peak[at] = top
            mass = functools.reduce(jnp.add, groups)
            part = dot(jnp.concatenate(groups, 1).astype(BF16), vv, 1, 0)
            if index:
                shrink = jnp.exp2(old - top)
                mass = mass + norm[at] * shrink
                part = part + acc[at] * shrink
            norm[at] = mass
            acc[at] = part
            dp[at, low : low + count] = dot(dos[at], vv, 1, 1)

    def score_clean(side, part):
        low = column(side, part)
        place = lax.broadcasted_iota(jnp.int32, (1, width), 1) // BLK
        dead = jnp.zeros((1, width), F32)
        for j in range(half):
            p = part * half + j
            b = block_of(side, p)
            for i, dst in enumerate((keys, values)):
                both = kv[side, p, i].astype(F32).reshape(2 * BLK, kw)
                dst[low + j * BLK : low + (j + 1) * BLK] = jnp.where(b == 1, both[BLK:], both[:BLK]).astype(BF16)
            dead = jnp.where(place == j, jnp.where(b < 0, -1e30, 0.0), dead)
        bias[:, low : low + width] = dead
        score(1 + 2 * side + part)

    def take_rows():
        for copy in sum(noisy + other_noisy, []) + sum(wide, []):
            copy.wait_recv()
        for copy in back:
            copy.wait()
        pulls = [
            pltpu.make_async_copy(src, dst, load_sem.at[i])
            for i, (src, dst) in enumerate(
                ((qg, q_all), (dog, do_all), (kn, keys.at[0:span]), (vn, values.at[0:span]))
            )
        ]
        for copy in pulls:
            copy.start()
        for copy in pulls:
            copy.wait()
        for r in range(heads):
            at, col = slice(r * rows, (r + 1) * rows), slice(r * HEAD_SIZE, (r + 1) * HEAD_SIZE)
            qs[at] = q_all[:, col]
            dos[at] = do_all[:, col]

    rounds = [[(0, 0)]]
    for near in range(1, me.right + 1, 2):
        rounds.append([(w, far) for far in (near + 1, near) for w in (0, 1) if far <= reach[w]])

    def advance(r):
        if r == 0:
            for stride in (2, 1):
                for i in (0, 1):
                    for w in (0, 1):
                        if stride <= reach[w]:
                            hop(w, 0, stride, i)
            pass_on(source(0, 0))
            return
        for begin in range(0, len(rounds[r]), 2):
            group = rounds[r][begin : begin + 2]
            for i in (0, 1):
                for direction, far in group:
                    arriving[direction, far, i].wait_recv()
                    if far + 2 <= reach[direction]:
                        hop(direction, far, 2, i)
            for unit in group:
                pass_on(source(*unit))

    def hand_round(r):
        for unit in rounds[r]:
            hand_over(source(*unit))

    advance(0)
    for copy in pair_kv:
        copy.wait_recv()
    other_noisy = [
        spread(6 + i, src, lambda j, dst=dst: dst.at[pl.ds(pl.multiple_of(rows + j * few, 8), few)], kw)
        for i, (src, dst) in enumerate(((kp, kn), (vp, vn)))
    ]
    for i, (src, dst) in enumerate(((kp, own_kp), (vp, own_vp))):
        local.append(pltpu.make_async_copy(src.at[:, lanes(mine, kw)], dst, own_sem.at[6 + i]))
        local[-1].start()
    advance(1)
    for copy in local[2:]:
        copy.wait()
    back = [
        pltpu.make_async_copy(src, dst, own_sem.at[i])
        for i, (src, dst) in enumerate(
            (
                (own_k, kn.at[token_rows(mine)]),
                (own_v, vn.at[token_rows(mine)]),
                (own_q, qg.at[token_rows(mine)]),
                (own_do, dog.at[token_rows(mine)]),
                (own_kp, kn.at[pl.ds(pl.multiple_of(rows + mine * few, 8), few)]),
                (own_vp, vn.at[pl.ds(pl.multiple_of(rows + mine * few, 8), few)]),
            )
        )
    ]
    for copy in back:
        copy.start()
    listing.wait()
    take_rows()
    advance(2)
    hand_round(0)
    score(0)
    hand_round(1)
    score_clean(OWN, 0)
    advance(3)
    hand_round(2)
    score_clean(RIGHT, 0)
    advance(4)
    score_clean(LEFT, 0)
    hand_round(3)
    score_clean(OWN, 1)
    for p in range(half):
        across[p].wait_recv()
    score_clean(FAR, 0)
    hand_round(4)
    score_clean(RIGHT, 1)
    score_clean(LEFT, 1)
    for p in range(half, nz):
        across[p].wait_recv()
    score_clean(FAR, 1)

    def finish(r):
        at = slice(r * rows, (r + 1) * rows)
        col = slice(r * HEAD_SIZE, (r + 1) * HEAD_SIZE)
        top, inverse = peak[at], 1.0 / jnp.sum(norm[at], -1, keepdims=True)
        o = (acc[at] * inverse).astype(BF16)
        o_all[:, col] = o
        row_dot = jnp.sum(dos[at].astype(F32) * o.astype(F32), -1, keepdims=True)
        for index, (low, count) in enumerate(chunks):
            factor = jnp.exp2(tops[index, at] - top) * inverse
            for j in range(low, low + count, HEAD_SIZE):
                prob = t[at, j : j + HEAD_SIZE] * factor
                weights[at, j : j + HEAD_SIZE] = prob.astype(BF16)
                dscores[at, j : j + HEAD_SIZE] = (prob * (dp[at, j : j + HEAD_SIZE] - row_dot)).astype(BF16)
        dq_all[:, col] = (dot(dscores[at], keys[...], 1, 0) * SCALE).astype(BF16)

    for r in range(heads):
        finish(r)
    puts = [pltpu.make_async_copy(src, dst, put_sem.at[i]) for i, (src, dst) in enumerate(((o_all, og), (dq_all, dqg)))]
    for copy in puts:
        copy.start()

    def gradients(low, count):
        at = slice(low, low + count)
        return dot(qs[...], dscores[:, at], 0, 0).T * SCALE, dot(dos[...], weights[:, at], 0, 0).T

    def make_terms(side, part):
        for i, g in enumerate(gradients(column(side, part), width)):
            for j in range(half):
                terms[side, part * half + j, i] = g[j * BLK : (j + 1) * BLK].astype(BF16)

    def placed(value, whose, side, p):
        b = listed[me.wrap_x(whose) * nz + me.z, me.wrap_x(SIDES[side]) * nz + me.wrap_z(offsets[p])]
        value = value.astype(F32)
        return jnp.concatenate([jnp.where(b == block, value, 0.0) for block in (0, 1)], 0)

    rounds = []
    for step in range((me.right + 1) // 2):
        rounds.append([(w, reach[w] - 2 * step - i) for i in (0, 1) for w in (0, 1) if reach[w] - 2 * step - i > 0])
    rounds.append([(0, 0)])
    first, direct, second, flying = {}, {}, {}, {}

    def target(direction, far):
        return slot_of[far if direction == 0 else -far]

    def slots(r):
        return [target(*unit) for unit in rounds[r]] if r < len(rounds) else []

    def send_first(r):
        for p in slots(r):
            first[p] = go(
                remote(terms.at[FAR, p], relay_in.at[p], x_send.at[0, p], x_recv.at[0, p], me.x_peer(-1 if p % 2 else 1))
            )

    def send_direct(r):
        for p in slots(r):
            side, d = (RIGHT, 1) if p % 2 else (LEFT, -1)
            direct[p] = go(
                remote(terms.at[side, p], direct_in.at[p], x_send.at[1, p], x_recv.at[1, p], me.x_peer(d))
            )

    def send_second(r):
        for begin in (0, 2):
            group = slots(r)[begin : begin + 2]
            for p in group:
                first[p].wait_recv()
                side = LEFT if p % 2 else RIGHT
                for i in (0, 1):
                    relay_out[p, i] = (
                        placed(relay_in[p, i], 1 if p % 2 else -1, side, p) + placed(terms[side, p, i], 0, side, p)
                    ).astype(BF16)
            for p in group:
                second[p] = go(
                    remote(relay_out.at[p], second_in.at[p], x_send.at[2, p], x_recv.at[2, p], me.x_peer(-1 if p % 2 else 1))
                )

    def total(direction, far, i):
        p = target(direction, far)
        if i == 0:
            direct[p].wait_recv()
            second[p].wait_recv()
        value = (
            placed(terms[OWN, p, i], 0, OWN, p)
            + placed(direct_in[p, i], -1 if p % 2 else 1, OWN, p)
            + second_in[p, i].astype(F32)
        )
        before = [(direction, far + 2)] if far else [(w, f) for f in (1, 2) for w in (0, 1)]
        for w, f in before:
            if f <= reach[w]:
                flying[w, f, i].wait_recv()
                value = value + ring_in[w, f, i].astype(F32)
        return value.astype(BF16)

    def send_ring(r):
        for begin in range(0, len(rounds[r]), 2):
            group = rounds[r][begin : begin + 2]
            for i in (0, 1):
                for direction, far in group:
                    ring_out[direction, far, i] = total(direction, far, i)
                for direction, far in group:
                    stride = min(2, far)
                    flying[direction, far, i] = go(
                        remote(
                            ring_out.at[direction, far, i], ring_in.at[direction, far, i],
                            z_send.at[direction, far, i], z_recv.at[direction, far, i],
                            me.z_peer(stride if direction == 0 else -stride),
                        )
                    )

    def head_out(which, src_at, dst, size):
        copies = []
        for d in range(1, nh):
            copies.append(
                go(
                    remote(
                        src_at(me.wrap_head(d)), dst.at[:, lanes(mine, size)],
                        out_send.at[which, d], out_recv.at[which, d], me.head_peer(d),
                    )
                )
            )
        return copies

    results = []
    make_terms(FAR, 1)
    send_first(0)
    send_first(1)
    make_terms(RIGHT, 1)
    make_terms(LEFT, 1)
    send_direct(0)
    make_terms(OWN, 1)
    for copy in puts:
        copy.wait()
    mids = [
        pltpu.make_async_copy(og.at[token_rows(mine)], own_q, own_sem.at[0]),
        pltpu.make_async_copy(dqg.at[token_rows(mine)], own_do, own_sem.at[1]),
    ]
    for copy in mids:
        copy.start()
    for i, (src, dst) in enumerate(((og, o_out), (dqg, dq_out))):
        results += head_out(i, lambda j, src=src: src.at[token_rows(j)], dst, qw)
    for i, g in enumerate(gradients(0, span)):
        span_grad[i] = g[0:rows]
        other[i] = g[rows:span].astype(BF16)
    send_second(0)
    send_direct(1)
    pair = [
        go(remote(other.at[i], pair_in.at[i], pair_send.at[i], pair_recv.at[i], me.partner(mine))) for i in (0, 1)
    ]
    make_terms(FAR, 0)
    send_first(2)
    make_terms(RIGHT, 0)
    make_terms(LEFT, 0)
    send_second(1)
    send_direct(2)
    send_first(3)
    send_ring(0)
    make_terms(OWN, 0)
    for copy in mids:
        copy.wait()
    mids = [
        pltpu.make_async_copy(own_q, o_out.at[:, lanes(mine, qw)], own_sem.at[0]),
        pltpu.make_async_copy(own_do, dq_out.at[:, lanes(mine, qw)], own_sem.at[1]),
    ]
    for copy in mids:
        copy.start()
    for i in (0, 1):
        pair[i].wait_recv()
        noisy_sum[i] = (span_grad[i] + pair_in[i].astype(F32)).astype(BF16)
    put = pltpu.make_async_copy(noisy_sum, ng, put_sem.at[0])
    put.start()
    for r in range(1, len(rounds)):
        if r > 1:
            send_direct(r + 1)
            send_first(r + 2)
        if r + 1 < len(rounds) or r == 1:
            send_second(r + 1)
        if r == len(rounds) - 1:
            break
        send_ring(r)
        if r == 1:
            put.wait()
            tail = [pltpu.make_async_copy(ng.at[i, token_rows(mine)], ref, own_sem.at[2 + i]) for i, ref in enumerate((own_k, own_v))]
            for copy in tail:
                copy.start()
            for i, dst in enumerate((dk_out, dv_out)):
                results += head_out(2 + i, lambda j, i=i: ng.at[i, token_rows(j)], dst, kw)
            for copy in tail:
                copy.wait()
            for i, (ref, dst) in enumerate(((own_k, dk_out), (own_v, dv_out))):
                mids.append(pltpu.make_async_copy(ref, dst.at[:, lanes(mine, kw)], own_sem.at[2 + i]))
                mids[-1].start()
    for i, dst in enumerate((dck_out, dcv_out)):
        final[i] = total(0, 0, i).astype(F32).reshape(final.shape[1:]).astype(BF16)
    for i, dst in enumerate((dck_out, dcv_out)):
        results += head_out(4 + i, lambda j, i=i: final.at[i, j], dst, kw)
        mids.append(pltpu.make_async_copy(final.at[i, mine], dst.at[:, lanes(mine, kw)], own_sem.at[4 + i]))
        mids[-1].start()
    for copy in results:
        copy.wait_recv()
    for copy in sends:
        copy.wait_send()
    for copy in mids:
        copy.wait()


def everything(nz, nh, history, q, do, k, v, ck, cv):
    few, qw, kw, crows = q.shape[0], q.shape[1] // nh, k.shape[1] // nh, ck.shape[0]
    rows = few * nh
    span = 2 * rows
    count = span + NX * nz * BLK
    stacked = rows * (qw // HEAD_SIZE)
    half = nz // 2
    unit = (2, nh, crows, kw)
    dma = pltpu.SemaphoreType.DMA

    def shape(*dims):
        return jax.ShapeDtypeStruct(dims, BF16)

    return pl.pallas_call(
        functools.partial(kernel, nz, nh),
        out_shape=(
            shape(few, nh * qw), shape(few, nh * qw), shape(few, nh * kw), shape(few, nh * kw),
            shape(crows, nh * kw), shape(crows, nh * kw),
            shape(rows, qw), shape(rows, qw), shape(span, kw), shape(span, kw),
            shape(rows, qw), shape(rows, qw), shape(2, rows, kw),
            shape(few, nh * kw), shape(few, nh * kw),
        ),
        in_specs=[ANY] * 7,
        out_specs=(ANY,) * 15,
        scratch_shapes=[
            pltpu.SMEM(history.shape, jnp.int32),
            pltpu.VMEM((NX, nz) + unit, BF16),
            pltpu.VMEM((few, qw), BF16),
            pltpu.VMEM((few, qw), BF16),
            pltpu.VMEM((few, kw), BF16),
            pltpu.VMEM((few, kw), BF16),
            pltpu.VMEM((few, kw), BF16),
            pltpu.VMEM((few, kw), BF16),
            pltpu.VMEM((rows, qw), BF16),
            pltpu.VMEM((rows, qw), BF16),
            pltpu.VMEM((rows, qw), BF16),
            pltpu.VMEM((rows, qw), BF16),
            pltpu.VMEM((stacked, kw), BF16),
            pltpu.VMEM((stacked, kw), BF16),
            pltpu.VMEM((count, kw), BF16),
            pltpu.VMEM((count, kw), BF16),
            pltpu.VMEM((stacked, count), F32),
            pltpu.VMEM((stacked, count), F32),
            pltpu.VMEM((9, stacked, HEAD_SIZE), F32),
            pltpu.VMEM((stacked, HEAD_SIZE), F32),
            pltpu.VMEM((stacked, HEAD_SIZE), F32),
            pltpu.VMEM((stacked, HEAD_SIZE), F32),
            pltpu.VMEM((stacked, count), BF16),
            pltpu.VMEM((stacked, count), BF16),
            pltpu.VMEM((1, count), F32),
            pltpu.VMEM((NX, nz, 2, BLK, kw), BF16),
            pltpu.VMEM((nz, 2, BLK, kw), BF16),
            pltpu.VMEM((nz, 2, 2 * BLK, kw), BF16),
            pltpu.VMEM((nz, 2, BLK, kw), BF16),
            pltpu.VMEM((nz, 2, 2 * BLK, kw), BF16),
            pltpu.VMEM((2, half + 1, 2, 2 * BLK, kw), BF16),
            pltpu.VMEM((2, half + 1, 2, 2 * BLK, kw), BF16),
            pltpu.VMEM((2, rows, kw), BF16),
            pltpu.VMEM((2, rows, kw), BF16),
            pltpu.VMEM((2, rows, kw), F32),
            pltpu.VMEM((2, rows, kw), BF16),
            pltpu.VMEM(unit, BF16),
            dma, dma((8, nh)), dma((8, nh)), dma((8,)), dma((4,)),
            dma((2, half + 1, 2)), dma((2, half + 1, 2)), dma((3, nz)), dma((3, nz)),
            dma((6, nh)), dma((6, nh)), dma((2,)), dma((2,)), dma((2,)),
            dma((3, nz)), dma((3, nz)), dma((2, half + 1, 2)), dma((2, half + 1, 2)),
        ],
        compiler_params=pltpu.CompilerParams(
            collective_id=0, has_side_effects=True, vmem_limit_bytes=60 * 2**20
        ),
        name="everything",
    )(history, q, do, k, v, ck, cv)


def settle_kernel(*refs):
    count = len(refs) // 3
    ins, outs, held = refs[:count], refs[count : 2 * count], refs[2 * count : 3 * count]
    sem = refs[3 * count]
    loads = [pltpu.make_async_copy(a, b, sem.at[0, i]) for i, (a, b) in enumerate(zip(ins, held))]
    stores = [pltpu.make_async_copy(a, b, sem.at[1, i]) for i, (a, b) in enumerate(zip(held, outs))]
    for copy in loads:
        copy.start()
    for load, store in zip(loads, stores):
        load.wait()
        store.start()
    for copy in stores:
        copy.wait()


def settle(arrays):
    shapes = [(a.shape, a.dtype) for a in arrays]
    return pl.pallas_call(
        settle_kernel,
        out_shape=tuple(jax.ShapeDtypeStruct(*s) for s in shapes),
        in_specs=[ANY] * len(arrays),
        out_specs=(ANY,) * len(arrays),
        scratch_shapes=[pltpu.VMEM(*s) for s in shapes]
        + [pltpu.SemaphoreType.DMA((2, len(arrays)))] ,
        name="settle",
    )(*arrays)


def shards(nz, nh, queries, nk, nv, ck, cv, output_gradient, history_list):
    results = everything(nz, nh, history_list, queries, output_gradient, nk, nv, ck, cv)
    return settle(results[:6])


def solution(mesh):
    nz, nh = mesh.shape["ctx"] // NX, mesh.shape["head"]
    tokens = P(("ctx", "head"), None)
    return jax.shard_map(
        functools.partial(shards, nz, nh),
        mesh=mesh,
        in_specs=(tokens,) * 6 + (P(),),
        out_specs=(tokens,) * 6,
        check_vma=False,
    )
```

```python
import functools

import jax
import jax.numpy as jnp
from jax import lax
from jax.experimental import pallas as pl
from jax.experimental.pallas import tpu as pltpu
from jax.sharding import PartitionSpec as P

BLK = 32
HEAD_SIZE = 128
SCALE = HEAD_SIZE**-0.5
LOG2E = 1.4426950408889634
NX = 4
F32 = jnp.float32
BF16 = jnp.bfloat16
MESH = pl.DeviceIdType.MESH
ANY = pl.BlockSpec(memory_space=pl.ANY)
VMEM = pl.BlockSpec(memory_space=pltpu.VMEM)
SMEM = pl.BlockSpec(memory_space=pltpu.SMEM)


class Place:
    def __init__(self, nz, nh):
        self.nz, self.nh = nz, nh
        ctx = lax.axis_index("ctx")
        self.head = lax.axis_index("head")
        self.x = ctx // nz
        self.z = ctx % nz
        self.right = nz // 2
        self.left = nz - 1 - nz // 2

    def wrap_x(self, d):
        return lax.rem(self.x + (d + NX), NX)

    def wrap_z(self, d):
        return lax.rem(self.z + (d + self.nz), self.nz)

    def wrap_head(self, d):
        return lax.rem(self.head + (d + self.nh), self.nh)

    def at(self, x, z, head):
        return (x * self.nz + z, head)

    def x_peer(self, d):
        return self.at(self.wrap_x(d), self.z, self.head)

    def z_peer(self, d):
        return self.at(self.x, self.wrap_z(d), self.head)

    def head_peer(self, d):
        return self.at(self.x, self.z, self.wrap_head(d))

    def z_peers(self):
        return [self.z_peer(d) for d in (1, -1) + ((2, -2) if self.right > 1 else ())]

    def partner_z(self):
        return self.z + 1 - 2 * lax.rem(self.z, 2)

    def partner(self, head):
        return self.at(self.x, self.partner_z(), head)


def greet(peers):
    barrier = pltpu.get_barrier_semaphore()
    for peer in peers:
        pl.semaphore_signal(barrier, inc=1, device_id=peer, device_id_type=MESH)
    pl.semaphore_wait(barrier, len(peers))


def remote(src, dst, send, recv, peer):
    return pltpu.make_async_remote_copy(
        src_ref=src, dst_ref=dst, send_sem=send, recv_sem=recv, device_id=peer, device_id_type=MESH
    )


def lanes(index, width):
    return pl.ds(pl.multiple_of(index * width, 128), width)


def dot(a, b, dim_a, dim_b):
    return lax.dot_general(a, b, (((dim_a,), (dim_b,)), ((), ())), preferred_element_type=F32)


SIDES = (0, 1, -1, 2)
OWN, RIGHT, LEFT, FAR = range(4)


def kernel(
    nz, nh, history, q, do, k, v, ck, cv,
    o_out, dq_out, dk_out, dv_out, dck_out, dcv_out, qg, dog, kn, vn, og, dqg, ng, kp, vp,
    listed, kv, own_q, own_do, own_k, own_v, own_kp, own_vp, q_all, do_all, o_all, dq_all, qs, dos, keys, values,
    t, dp, tops, peak, norm, acc, weights, dscores, bias, terms, side_in, far_in, ring_in, ring_out,
    other, pair_in, span_grad, noisy_sum, final,
    list_sem, in_send, in_recv, own_sem, load_sem, gz_send, gz_recv, gx_send, gx_recv,
    out_send, out_recv, put_sem, pair_send, pair_recv, x_send, x_recv, z_send, z_recv,
):
    me = Place(nz, nh)
    mine = me.head
    qw, kw = q.shape[1] // nh, k.shape[1] // nh
    few = q.shape[0]
    rows = few * nh
    span = 2 * rows
    heads = qw // HEAD_SIZE
    half = nz // 2
    width = half * BLK
    reach = (me.right, me.left)
    offsets = [0] + [d * sign for d in range(1, half) for sign in (1, -1)] + [half]
    slot_of = {off: p for p, off in enumerate(offsets)}
    slot_of[-half] = slot_of[half]

    sends = []

    def go(copy):
        copy.start()
        sends.append(copy)
        return copy

    def token_rows(index):
        return pl.ds(pl.multiple_of(index * few, 8), few)

    ctx = lax.axis_index("ctx")
    listing = pltpu.make_async_copy(history, listed, list_sem)
    listing.start()
    local = [
        pltpu.make_async_copy(ck.at[:, lanes(mine, kw)], kv.at[OWN, 0, 0, mine], own_sem.at[0]),
        pltpu.make_async_copy(cv.at[:, lanes(mine, kw)], kv.at[OWN, 0, 1, mine], own_sem.at[1]),
        pltpu.make_async_copy(k.at[:, lanes(mine, kw)], own_k, own_sem.at[2]),
        pltpu.make_async_copy(v.at[:, lanes(mine, kw)], own_v, own_sem.at[3]),
        pltpu.make_async_copy(q.at[:, lanes(mine, qw)], own_q, own_sem.at[4]),
        pltpu.make_async_copy(do.at[:, lanes(mine, qw)], own_do, own_sem.at[5]),
    ]
    for copy in local:
        copy.start()
    greet([me.head_peer(d) for d in range(1, nh)] + me.z_peers() + [me.x_peer(1), me.x_peer(-1), me.x_peer(2)])

    def spread(which, src, dst_at, size):
        copies = []
        for d in range(1, nh):
            copies.append(
                go(
                    remote(
                        src.at[:, lanes(me.wrap_head(d), size)], dst_at(mine),
                        in_send.at[which, d], in_recv.at[which, d], me.head_peer(d),
                    )
                )
            )
        return copies

    clean = [spread(i, src, lambda j, i=i: kv.at[OWN, 0, i, j], kw) for i, src in enumerate((ck, cv))]
    noisy = [spread(2 + i, src, lambda j, dst=dst: dst.at[token_rows(j)], kw) for i, (src, dst) in enumerate(((k, kn), (v, vn)))]
    wide = [spread(4 + i, src, lambda j, dst=dst: dst.at[token_rows(j)], qw) for i, (src, dst) in enumerate(((q, qg), (do, dog)))]
    pair_kv = [
        go(remote(src, dst, in_send.at[6 + i, 0], in_recv.at[6 + i, 0], me.partner(mine)))
        for i, (src, dst) in enumerate(((k, kp), (v, vp)))
    ]
    for copy in local[:2]:
        copy.wait()
    for copy in sum(clean, []):
        copy.wait_recv()

    arriving, sideways, across = {}, {}, {}

    def source(direction, far):
        return slot_of[-far if direction == 0 else far]

    def hop(direction, far, stride, i):
        arriving[direction, far + stride, i] = go(
            remote(
                kv.at[OWN, source(direction, far), i], kv.at[OWN, source(direction, far + stride), i],
                gz_send.at[direction, far + stride, i], gz_recv.at[direction, far + stride, i],
                me.z_peer(stride if direction == 0 else -stride),
            )
        )

    def pass_on(p):
        for i, (d, side) in enumerate(((1, LEFT), (-1, RIGHT))):
            sideways[p, i] = go(
                remote(kv.at[OWN, p], kv.at[side, p], gx_send.at[i, p], gx_recv.at[i, p], me.x_peer(d))
            )

    def hand_over(p):
        for i in (0, 1):
            sideways[p, i].wait_recv()
        side, d = (RIGHT, -1) if p % 2 else (LEFT, 1)
        across[p] = go(remote(kv.at[side, p], kv.at[FAR, p], gx_send.at[2, p], gx_recv.at[2, p], me.x_peer(d)))

    def block_of(side, p):
        return listed[ctx, me.wrap_x(SIDES[side]) * nz + me.wrap_z(offsets[p])]

    def column(side, part):
        return span + side * nz * BLK + part * width

    chunks = [(0, span)] + [(column(side, part), width) for side in range(NX) for part in (0, 1)]

    batches = ((0, 1), (3, 5), (2, 7), (4, 6, 8))

    def score(batch):
        for r in range(heads):
            at = slice(r * rows, (r + 1) * rows)
            groups = []
            for index in batches[batch]:
                low, count = chunks[index]
                s = dot(qs[at], keys[low : low + count], 1, 1) * (SCALE * LOG2E)
                if index:
                    s = s + bias[:, low : low + count]
                groups += [(low + j, s[:, j : j + HEAD_SIZE]) for j in range(0, count, HEAD_SIZE)]
            most = jnp.max(functools.reduce(jnp.maximum, [g for _, g in groups]), -1, keepdims=True)
            if batch:
                old = peak[at]
                top = jnp.maximum(old, most)
            else:
                top = jnp.broadcast_to(most, (rows, HEAD_SIZE))
            groups = [(j, jnp.exp2(g - top)) for j, g in groups]
            for j, g in groups:
                t[at, j : j + HEAD_SIZE] = g
            tops[batch, at] = top
            peak[at] = top
            mass = functools.reduce(jnp.add, [g for _, g in groups])
            if batch:
                shrink = jnp.exp2(old - top)
                mass = mass + norm[at] * shrink
                part = acc[at] * shrink
            else:
                part = jnp.zeros((rows, HEAD_SIZE), F32)
            for index in batches[batch]:
                low, count = chunks[index]
                e = jnp.concatenate([g for j, g in groups if low <= j < low + count], 1).astype(BF16)
                part = part + dot(e, values[low : low + count], 1, 0)
                dp[at, low : low + count] = dot(dos[at], values[low : low + count], 1, 1)
            norm[at] = mass
            acc[at] = part

    def listed_rows(side, part):
        low = column(side, part)
        place = lax.broadcasted_iota(jnp.int32, (1, width), 1) // BLK
        dead = jnp.zeros((1, width), F32)
        for j in range(half):
            p = part * half + j
            b = block_of(side, p)
            for i, dst in enumerate((keys, values)):
                both = kv[side, p, i].astype(F32).reshape(2 * BLK, kw)
                dst[low + j * BLK : low + (j + 1) * BLK] = jnp.where(b == 1, both[BLK:], both[:BLK]).astype(BF16)
            dead = jnp.where(place == j, jnp.where(b < 0, -1e30, 0.0), dead)
        bias[:, low : low + width] = dead

    def take_rows():
        for copy in sum(noisy + other_noisy, []) + sum(wide, []):
            copy.wait_recv()
        for copy in back:
            copy.wait()
        pulls = [
            pltpu.make_async_copy(src, dst, load_sem.at[i])
            for i, (src, dst) in enumerate(
                ((qg, q_all), (dog, do_all), (kn, keys.at[0:span]), (vn, values.at[0:span]))
            )
        ]
        for copy in pulls:
            copy.start()
        for copy in pulls:
            copy.wait()
        for r in range(heads):
            at, col = slice(r * rows, (r + 1) * rows), slice(r * HEAD_SIZE, (r + 1) * HEAD_SIZE)
            qs[at] = q_all[:, col]
            dos[at] = do_all[:, col]

    rounds = [[(0, 0)]]
    for near in range(1, me.right + 1, 2):
        rounds.append([(w, far) for far in (near + 1, near) for w in (0, 1) if far <= reach[w]])

    def advance(r):
        if r == 0:
            for stride in (2, 1):
                for i in (0, 1):
                    for w in (0, 1):
                        if stride <= reach[w]:
                            hop(w, 0, stride, i)
            pass_on(source(0, 0))
            return
        for begin in range(0, len(rounds[r]), 2):
            group = rounds[r][begin : begin + 2]
            for i in (0, 1):
                for direction, far in group:
                    arriving[direction, far, i].wait_recv()
                    if far + 2 <= reach[direction]:
                        hop(direction, far, 2, i)
            for unit in group:
                p = source(*unit)
                pass_on(p)
                if r == len(rounds) - 1:
                    across[p] = go(
                        remote(kv.at[OWN, p], kv.at[FAR, p], gx_send.at[2, p], gx_recv.at[2, p], me.x_peer(2))
                    )

    def hand_round(r):
        for unit in rounds[r]:
            hand_over(source(*unit))

    advance(0)
    for copy in pair_kv:
        copy.wait_recv()
    other_noisy = [
        spread(6 + i, src, lambda j, dst=dst: dst.at[pl.ds(pl.multiple_of(rows + j * few, 8), few)], kw)
        for i, (src, dst) in enumerate(((kp, kn), (vp, vn)))
    ]
    for i, (src, dst) in enumerate(((kp, own_kp), (vp, own_vp))):
        local.append(pltpu.make_async_copy(src.at[:, lanes(mine, kw)], dst, own_sem.at[6 + i]))
        local[-1].start()
    advance(1)
    for copy in local[2:]:
        copy.wait()
    back = [
        pltpu.make_async_copy(src, dst, own_sem.at[i])
        for i, (src, dst) in enumerate(
            (
                (own_k, kn.at[token_rows(mine)]),
                (own_v, vn.at[token_rows(mine)]),
                (own_q, qg.at[token_rows(mine)]),
                (own_do, dog.at[token_rows(mine)]),
                (own_kp, kn.at[pl.ds(pl.multiple_of(rows + mine * few, 8), few)]),
                (own_vp, vn.at[pl.ds(pl.multiple_of(rows + mine * few, 8), few)]),
            )
        )
    ]
    for copy in back:
        copy.start()
    listing.wait()
    take_rows()
    advance(2)
    hand_round(0)
    listed_rows(OWN, 0)
    score(0)
    hand_round(1)
    advance(3)
    hand_round(2)
    listed_rows(RIGHT, 0)
    listed_rows(LEFT, 0)
    advance(4)
    score(1)
    hand_round(3)
    listed_rows(OWN, 1)
    for p in range(half):
        across[p].wait_recv()
    listed_rows(FAR, 0)
    score(2)
    for unit in rounds[4]:
        for i in (0, 1):
            sideways[source(*unit), i].wait_recv()
    listed_rows(RIGHT, 1)
    listed_rows(LEFT, 1)
    for p in range(half, nz):
        across[p].wait_recv()
    listed_rows(FAR, 1)
    score(3)

    def finish(r):
        at = slice(r * rows, (r + 1) * rows)
        col = slice(r * HEAD_SIZE, (r + 1) * HEAD_SIZE)
        top, inverse = peak[at], 1.0 / jnp.sum(norm[at], -1, keepdims=True)
        o = (acc[at] * inverse).astype(BF16)
        o_all[:, col] = o
        row_dot = jnp.sum(dos[at].astype(F32) * o.astype(F32), -1, keepdims=True)
        for batch, indexes in enumerate(batches):
            factor = jnp.exp2(tops[batch, at] - top) * inverse
            for j in [j for low, count in (chunks[i] for i in indexes) for j in range(low, low + count, HEAD_SIZE)]:
                prob = t[at, j : j + HEAD_SIZE] * factor
                weights[at, j : j + HEAD_SIZE] = prob.astype(BF16)
                dscores[at, j : j + HEAD_SIZE] = (prob * (dp[at, j : j + HEAD_SIZE] - row_dot)).astype(BF16)
        dq_all[:, col] = (dot(dscores[at], keys[...], 1, 0) * SCALE).astype(BF16)

    for r in range(heads):
        finish(r)
    puts = [pltpu.make_async_copy(src, dst, put_sem.at[i]) for i, (src, dst) in enumerate(((o_all, og), (dq_all, dqg)))]
    for copy in puts:
        copy.start()

    def gradients(low, count):
        at = slice(low, low + count)
        return dot(qs[...], dscores[:, at], 0, 0).T * SCALE, dot(dos[...], weights[:, at], 0, 0).T

    def make_terms(side, part):
        for i, g in enumerate(gradients(column(side, part), width)):
            for j in range(half):
                terms[side, part * half + j, i] = g[j * BLK : (j + 1) * BLK].astype(BF16)

    def placed(value, whose, p):
        b = listed[me.wrap_x(whose) * nz + me.z, me.x * nz + me.wrap_z(offsets[p])]
        value = value.astype(F32)
        return jnp.concatenate([jnp.where(b == block, value, 0.0) for block in (0, 1)], 0)

    rounds = []
    for step in range((me.right + 1) // 2):
        rounds.append([(w, reach[w] - 2 * step - i) for i in (0, 1) for w in (0, 1) if reach[w] - 2 * step - i > 0])
    rounds.append([(0, 0)])
    beside, opposite, flying = {}, {}, {}

    def target(direction, far):
        return slot_of[far if direction == 0 else -far]

    def slots(r):
        return [target(*unit) for unit in rounds[r]] if r < len(rounds) else []

    def send_opposite(r):
        for p in slots(r):
            opposite[p] = go(
                remote(terms.at[FAR, p], far_in.at[p], x_send.at[2, p], x_recv.at[2, p], me.x_peer(2))
            )

    def send_beside(r):
        for p in slots(r):
            for i, (side, d) in enumerate(((RIGHT, 1), (LEFT, -1))):
                beside[p, i] = go(
                    remote(terms.at[side, p], side_in.at[i, p], x_send.at[i, p], x_recv.at[i, p], me.x_peer(d))
                )

    def total(direction, far, i):
        p = target(direction, far)
        if i == 0:
            beside[p, 0].wait_recv()
            beside[p, 1].wait_recv()
            opposite[p].wait_recv()
        value = (
            placed(terms[OWN, p, i], 0, p)
            + placed(side_in[0, p, i], -1, p)
            + placed(side_in[1, p, i], 1, p)
            + placed(far_in[p, i], 2, p)
        )
        before = [(direction, far + 2)] if far else [(w, f) for f in (1, 2) for w in (0, 1)]
        for w, f in before:
            if f <= reach[w]:
                flying[w, f, i].wait_recv()
                value = value + ring_in[w, f, i].astype(F32)
        return value.astype(BF16)

    def send_ring(r):
        for begin in range(0, len(rounds[r]), 2):
            group = rounds[r][begin : begin + 2]
            for i in (0, 1):
                for direction, far in group:
                    ring_out[direction, far, i] = total(direction, far, i)
                for direction, far in group:
                    stride = min(2, far)
                    flying[direction, far, i] = go(
                        remote(
                            ring_out.at[direction, far, i], ring_in.at[direction, far, i],
                            z_send.at[direction, far, i], z_recv.at[direction, far, i],
                            me.z_peer(stride if direction == 0 else -stride),
                        )
                    )

    def head_out(which, src_at, dst, size):
        copies = []
        for d in range(1, nh):
            copies.append(
                go(
                    remote(
                        src_at(me.wrap_head(d)), dst.at[:, lanes(mine, size)],
                        out_send.at[which, d], out_recv.at[which, d], me.head_peer(d),
                    )
                )
            )
        return copies

    results = []
    make_terms(FAR, 1)
    send_opposite(0)
    make_terms(RIGHT, 1)
    make_terms(LEFT, 1)
    send_beside(0)
    send_opposite(1)
    send_beside(1)
    make_terms(OWN, 1)
    for copy in puts:
        copy.wait()
    mids = [
        pltpu.make_async_copy(og.at[token_rows(mine)], own_q, own_sem.at[0]),
        pltpu.make_async_copy(dqg.at[token_rows(mine)], own_do, own_sem.at[1]),
    ]
    for copy in mids:
        copy.start()
    for i, (src, dst) in enumerate(((og, o_out), (dqg, dq_out))):
        results += head_out(i, lambda j, src=src: src.at[token_rows(j)], dst, qw)
    for i, g in enumerate(gradients(0, span)):
        span_grad[i] = g[0:rows]
        other[i] = g[rows:span].astype(BF16)
    pair = [
        go(remote(other.at[i], pair_in.at[i], pair_send.at[i], pair_recv.at[i], me.partner(mine))) for i in (0, 1)
    ]
    make_terms(FAR, 0)
    make_terms(RIGHT, 0)
    make_terms(LEFT, 0)
    for r in (2, 3, 4):
        send_opposite(r)
        send_beside(r)
    make_terms(OWN, 0)
    send_ring(0)
    for copy in mids:
        copy.wait()
    mids = [
        pltpu.make_async_copy(own_q, o_out.at[:, lanes(mine, qw)], own_sem.at[0]),
        pltpu.make_async_copy(own_do, dq_out.at[:, lanes(mine, qw)], own_sem.at[1]),
    ]
    for copy in mids:
        copy.start()
    for i in (0, 1):
        pair[i].wait_recv()
        noisy_sum[i] = (span_grad[i] + pair_in[i].astype(F32)).astype(BF16)
    put = pltpu.make_async_copy(noisy_sum, ng, put_sem.at[0])
    put.start()
    for r in range(1, len(rounds)):
        if r == len(rounds) - 1:
            break
        send_ring(r)
        if r == 1:
            put.wait()
            tail = [pltpu.make_async_copy(ng.at[i, token_rows(mine)], ref, own_sem.at[2 + i]) for i, ref in enumerate((own_k, own_v))]
            for copy in tail:
                copy.start()
            for i, dst in enumerate((dk_out, dv_out)):
                results += head_out(2 + i, lambda j, i=i: ng.at[i, token_rows(j)], dst, kw)
            for copy in tail:
                copy.wait()
            for i, (ref, dst) in enumerate(((own_k, dk_out), (own_v, dv_out))):
                mids.append(pltpu.make_async_copy(ref, dst.at[:, lanes(mine, kw)], own_sem.at[2 + i]))
                mids[-1].start()
    for i, dst in enumerate((dck_out, dcv_out)):
        final[i] = total(0, 0, i).astype(F32).reshape(final.shape[1:]).astype(BF16)
    for i, dst in enumerate((dck_out, dcv_out)):
        results += head_out(4 + i, lambda j, i=i: final.at[i, j], dst, kw)
        mids.append(pltpu.make_async_copy(final.at[i, mine], dst.at[:, lanes(mine, kw)], own_sem.at[4 + i]))
        mids[-1].start()
    for copy in results:
        copy.wait_recv()
    for copy in sends:
        copy.wait_send()
    for copy in mids:
        copy.wait()


def everything(nz, nh, history, q, do, k, v, ck, cv):
    few, qw, kw, crows = q.shape[0], q.shape[1] // nh, k.shape[1] // nh, ck.shape[0]
    rows = few * nh
    span = 2 * rows
    count = span + NX * nz * BLK
    stacked = rows * (qw // HEAD_SIZE)
    half = nz // 2
    unit = (2, nh, crows, kw)
    dma = pltpu.SemaphoreType.DMA

    def shape(*dims):
        return jax.ShapeDtypeStruct(dims, BF16)

    return pl.pallas_call(
        functools.partial(kernel, nz, nh),
        out_shape=(
            shape(few, nh * qw), shape(few, nh * qw), shape(few, nh * kw), shape(few, nh * kw),
            shape(crows, nh * kw), shape(crows, nh * kw),
            shape(rows, qw), shape(rows, qw), shape(span, kw), shape(span, kw),
            shape(rows, qw), shape(rows, qw), shape(2, rows, kw),
            shape(few, nh * kw), shape(few, nh * kw),
        ),
        in_specs=[ANY] * 7,
        out_specs=(ANY,) * 15,
        scratch_shapes=[
            pltpu.SMEM(history.shape, jnp.int32),
            pltpu.VMEM((NX, nz) + unit, BF16),
            pltpu.VMEM((few, qw), BF16),
            pltpu.VMEM((few, qw), BF16),
            pltpu.VMEM((few, kw), BF16),
            pltpu.VMEM((few, kw), BF16),
            pltpu.VMEM((few, kw), BF16),
            pltpu.VMEM((few, kw), BF16),
            pltpu.VMEM((rows, qw), BF16),
            pltpu.VMEM((rows, qw), BF16),
            pltpu.VMEM((rows, qw), BF16),
            pltpu.VMEM((rows, qw), BF16),
            pltpu.VMEM((stacked, kw), BF16),
            pltpu.VMEM((stacked, kw), BF16),
            pltpu.VMEM((count, kw), BF16),
            pltpu.VMEM((count, kw), BF16),
            pltpu.VMEM((stacked, count), F32),
            pltpu.VMEM((stacked, count), F32),
            pltpu.VMEM((4, stacked, HEAD_SIZE), F32),
            pltpu.VMEM((stacked, HEAD_SIZE), F32),
            pltpu.VMEM((stacked, HEAD_SIZE), F32),
            pltpu.VMEM((stacked, HEAD_SIZE), F32),
            pltpu.VMEM((stacked, count), BF16),
            pltpu.VMEM((stacked, count), BF16),
            pltpu.VMEM((1, count), F32),
            pltpu.VMEM((NX, nz, 2, BLK, kw), BF16),
            pltpu.VMEM((2, nz, 2, BLK, kw), BF16),
            pltpu.VMEM((nz, 2, BLK, kw), BF16),
            pltpu.VMEM((2, half + 1, 2, 2 * BLK, kw), BF16),
            pltpu.VMEM((2, half + 1, 2, 2 * BLK, kw), BF16),
            pltpu.VMEM((2, rows, kw), BF16),
            pltpu.VMEM((2, rows, kw), BF16),
            pltpu.VMEM((2, rows, kw), F32),
            pltpu.VMEM((2, rows, kw), BF16),
            pltpu.VMEM(unit, BF16),
            dma, dma((8, nh)), dma((8, nh)), dma((8,)), dma((4,)),
            dma((2, half + 1, 2)), dma((2, half + 1, 2)), dma((3, nz)), dma((3, nz)),
            dma((6, nh)), dma((6, nh)), dma((2,)), dma((2,)), dma((2,)),
            dma((3, nz)), dma((3, nz)), dma((2, half + 1, 2)), dma((2, half + 1, 2)),
        ],
        compiler_params=pltpu.CompilerParams(
            collective_id=0, has_side_effects=True, vmem_limit_bytes=60 * 2**20
        ),
        name="everything",
    )(history, q, do, k, v, ck, cv)


def settle_kernel(*refs):
    count = len(refs) // 3
    ins, outs, held = refs[:count], refs[count : 2 * count], refs[2 * count : 3 * count]
    sem = refs[3 * count]
    loads = [pltpu.make_async_copy(a, b, sem.at[0, i]) for i, (a, b) in enumerate(zip(ins, held))]
    stores = [pltpu.make_async_copy(a, b, sem.at[1, i]) for i, (a, b) in enumerate(zip(held, outs))]
    for copy in loads:
        copy.start()
    for load, store in zip(loads, stores):
        load.wait()
        store.start()
    for copy in stores:
        copy.wait()


def settle(arrays):
    shapes = [(a.shape, a.dtype) for a in arrays]
    return pl.pallas_call(
        settle_kernel,
        out_shape=tuple(jax.ShapeDtypeStruct(*s) for s in shapes),
        in_specs=[ANY] * len(arrays),
        out_specs=(ANY,) * len(arrays),
        scratch_shapes=[pltpu.VMEM(*s) for s in shapes]
        + [pltpu.SemaphoreType.DMA((2, len(arrays)))] ,
        name="settle",
    )(*arrays)


def shards(nz, nh, queries, nk, nv, ck, cv, output_gradient, history_list):
    results = everything(nz, nh, history_list, queries, output_gradient, nk, nv, ck, cv)
    return settle(results[:6])


def solution(mesh):
    nz, nh = mesh.shape["ctx"] // NX, mesh.shape["head"]
    tokens = P(("ctx", "head"), None)
    return jax.shard_map(
        functools.partial(shards, nz, nh),
        mesh=mesh,
        in_specs=(tokens,) * 6 + (P(),),
        out_specs=(tokens,) * 6,
        check_vma=False,
    )
```

```python
import functools

import jax
import jax.numpy as jnp
from jax import lax
from jax.experimental import pallas as pl
from jax.experimental.pallas import tpu as pltpu
from jax.sharding import PartitionSpec as P

BLK = 32
HEAD_SIZE = 128
SCALE = HEAD_SIZE**-0.5
LOG2E = 1.4426950408889634
NX = 4
F32 = jnp.float32
BF16 = jnp.bfloat16
MESH = pl.DeviceIdType.MESH
ANY = pl.BlockSpec(memory_space=pl.ANY)
VMEM = pl.BlockSpec(memory_space=pltpu.VMEM)
SMEM = pl.BlockSpec(memory_space=pltpu.SMEM)


class Place:
    def __init__(self, nz, nh):
        self.nz, self.nh = nz, nh
        ctx = lax.axis_index("ctx")
        self.head = lax.axis_index("head")
        self.x = ctx // nz
        self.z = ctx % nz
        self.right = nz // 2
        self.left = nz - 1 - nz // 2

    def wrap_x(self, d):
        return lax.rem(self.x + (d + NX), NX)

    def wrap_z(self, d):
        return lax.rem(self.z + (d + self.nz), self.nz)

    def wrap_head(self, d):
        return lax.rem(self.head + (d + self.nh), self.nh)

    def at(self, x, z, head):
        return (x * self.nz + z, head)

    def x_peer(self, d):
        return self.at(self.wrap_x(d), self.z, self.head)

    def z_peer(self, d):
        return self.at(self.x, self.wrap_z(d), self.head)

    def head_peer(self, d):
        return self.at(self.x, self.z, self.wrap_head(d))

    def z_peers(self):
        return [self.z_peer(d) for d in (1, -1) + ((2, -2) if self.right > 1 else ())]

    def partner_z(self):
        return self.z + 1 - 2 * lax.rem(self.z, 2)

    def partner(self, head):
        return self.at(self.x, self.partner_z(), head)


def greet(peers):
    barrier = pltpu.get_barrier_semaphore()
    for peer in peers:
        pl.semaphore_signal(barrier, inc=1, device_id=peer, device_id_type=MESH)
    pl.semaphore_wait(barrier, len(peers))


def remote(src, dst, send, recv, peer):
    return pltpu.make_async_remote_copy(
        src_ref=src, dst_ref=dst, send_sem=send, recv_sem=recv, device_id=peer, device_id_type=MESH
    )


def lanes(index, width):
    return pl.ds(pl.multiple_of(index * width, 128), width)


def dot(a, b, dim_a, dim_b):
    return lax.dot_general(a, b, (((dim_a,), (dim_b,)), ((), ())), preferred_element_type=F32)


SIDES = (0, 1, -1, 2)
OWN, RIGHT, LEFT, FAR = range(4)


def kernel(
    nz, nh, history, q, do, k, v, ck, cv,
    o_out, dq_out, dk_out, dv_out, dck_out, dcv_out, qg, dog, kn, vn, og, dqg, ng, kp, vp,
    listed, kv, own_q, own_do, own_k, own_v, own_kp, own_vp, q_all, do_all, o_all, dq_all, qs, dos, keys, values,
    t, dp, tops, peak, norm, acc, weights, dscores, bias, terms, side_in, far_in, ring_in, ring_out,
    other, pair_in, span_grad, noisy_sum, final,
    list_sem, in_send, in_recv, own_sem, load_sem, gz_send, gz_recv, gx_send, gx_recv,
    out_send, out_recv, put_sem, pair_send, pair_recv, x_send, x_recv, z_send, z_recv,
):
    me = Place(nz, nh)
    mine = me.head
    qw, kw = q.shape[1] // nh, k.shape[1] // nh
    few = q.shape[0]
    rows = few * nh
    span = 2 * rows
    heads = qw // HEAD_SIZE
    half = nz // 2
    width = half * BLK
    reach = (me.right, me.left)
    offsets = [0] + [d * sign for d in range(1, half) for sign in (1, -1)] + [half]
    slot_of = {off: p for p, off in enumerate(offsets)}
    slot_of[-half] = slot_of[half]

    sends = []

    def go(copy):
        copy.start()
        sends.append(copy)
        return copy

    def token_rows(index):
        return pl.ds(pl.multiple_of(index * few, 8), few)

    ctx = lax.axis_index("ctx")
    listing = pltpu.make_async_copy(history, listed, list_sem)
    listing.start()
    local = [
        pltpu.make_async_copy(ck.at[:, lanes(mine, kw)], kv.at[OWN, 0, 0, mine], own_sem.at[0]),
        pltpu.make_async_copy(cv.at[:, lanes(mine, kw)], kv.at[OWN, 0, 1, mine], own_sem.at[1]),
        pltpu.make_async_copy(k.at[:, lanes(mine, kw)], own_k, own_sem.at[2]),
        pltpu.make_async_copy(v.at[:, lanes(mine, kw)], own_v, own_sem.at[3]),
        pltpu.make_async_copy(q.at[:, lanes(mine, qw)], own_q, own_sem.at[4]),
        pltpu.make_async_copy(do.at[:, lanes(mine, qw)], own_do, own_sem.at[5]),
    ]
    for copy in local:
        copy.start()
    greet([me.head_peer(d) for d in range(1, nh)] + me.z_peers() + [me.x_peer(1), me.x_peer(-1), me.x_peer(2)])

    def spread(which, src, dst_at, size):
        copies = []
        for d in range(1, nh):
            copies.append(
                go(
                    remote(
                        src.at[:, lanes(me.wrap_head(d), size)], dst_at(mine),
                        in_send.at[which, d], in_recv.at[which, d], me.head_peer(d),
                    )
                )
            )
        return copies

    clean = [spread(i, src, lambda j, i=i: kv.at[OWN, 0, i, j], kw) for i, src in enumerate((ck, cv))]
    noisy = [spread(2 + i, src, lambda j, dst=dst: dst.at[token_rows(j)], kw) for i, (src, dst) in enumerate(((k, kn), (v, vn)))]
    wide = [spread(4 + i, src, lambda j, dst=dst: dst.at[token_rows(j)], qw) for i, (src, dst) in enumerate(((q, qg), (do, dog)))]
    pair_kv = [
        go(remote(src, dst, in_send.at[6 + i, 0], in_recv.at[6 + i, 0], me.partner(mine)))
        for i, (src, dst) in enumerate(((k, kp), (v, vp)))
    ]
    for copy in local[:2]:
        copy.wait()
    for copy in sum(clean, []):
        copy.wait_recv()

    arriving, sideways, across = {}, {}, {}

    def source(direction, far):
        return slot_of[-far if direction == 0 else far]

    def hop(direction, far, stride, i):
        arriving[direction, far + stride, i] = go(
            remote(
                kv.at[OWN, source(direction, far), i], kv.at[OWN, source(direction, far + stride), i],
                gz_send.at[direction, far + stride, i], gz_recv.at[direction, far + stride, i],
                me.z_peer(stride if direction == 0 else -stride),
            )
        )

    def pass_on(p):
        for i, (d, side) in enumerate(((1, LEFT), (-1, RIGHT))):
            sideways[p, i] = go(
                remote(kv.at[OWN, p], kv.at[side, p], gx_send.at[i, p], gx_recv.at[i, p], me.x_peer(d))
            )

    def hand_over(p):
        for i in (0, 1):
            sideways[p, i].wait_recv()
        side, d = (RIGHT, -1) if p % 2 else (LEFT, 1)
        across[p] = go(remote(kv.at[side, p], kv.at[FAR, p], gx_send.at[2, p], gx_recv.at[2, p], me.x_peer(d)))

    def block_of(side, p):
        return listed[ctx, me.wrap_x(SIDES[side]) * nz + me.wrap_z(offsets[p])]

    def column(side, part):
        return span + side * nz * BLK + part * width

    chunks = [(0, span)] + [(column(side, part), width) for side in range(NX) for part in (0, 1)]

    batches = ((0, 1), (3, 5), (2, 7), (4, 6, 8))

    def score(batch):
        for r in range(heads):
            at = slice(r * rows, (r + 1) * rows)
            groups = []
            for index in batches[batch]:
                low, count = chunks[index]
                s = dot(qs[at], keys[low : low + count], 1, 1) * (SCALE * LOG2E)
                if index:
                    s = s + bias[:, low : low + count]
                groups += [(low + j, s[:, j : j + HEAD_SIZE]) for j in range(0, count, HEAD_SIZE)]
            most = jnp.max(functools.reduce(jnp.maximum, [g for _, g in groups]), -1, keepdims=True)
            if batch:
                old = peak[at]
                top = jnp.maximum(old, most)
            else:
                top = jnp.broadcast_to(most, (rows, HEAD_SIZE))
            groups = [(j, jnp.exp2(g - top)) for j, g in groups]
            for j, g in groups:
                t[at, j : j + HEAD_SIZE] = g
            tops[batch, at] = top
            peak[at] = top
            mass = functools.reduce(jnp.add, [g for _, g in groups])
            if batch:
                shrink = jnp.exp2(old - top)
                mass = mass + norm[at] * shrink
                part = acc[at] * shrink
            else:
                part = jnp.zeros((rows, HEAD_SIZE), F32)
            for index in batches[batch]:
                low, count = chunks[index]
                e = jnp.concatenate([g for j, g in groups if low <= j < low + count], 1).astype(BF16)
                part = part + dot(e, values[low : low + count], 1, 0)
                dp[at, low : low + count] = dot(dos[at], values[low : low + count], 1, 1)
            norm[at] = mass
            acc[at] = part

    def listed_rows(side, part):
        low = column(side, part)
        place = lax.broadcasted_iota(jnp.int32, (1, width), 1) // BLK
        dead = jnp.zeros((1, width), F32)
        for j in range(half):
            p = part * half + j
            b = block_of(side, p)
            for i, dst in enumerate((keys, values)):
                both = kv[side, p, i].astype(F32).reshape(2 * BLK, kw)
                dst[low + j * BLK : low + (j + 1) * BLK] = jnp.where(b == 1, both[BLK:], both[:BLK]).astype(BF16)
            dead = jnp.where(place == j, jnp.where(b < 0, -1e30, 0.0), dead)
        bias[:, low : low + width] = dead

    def take_rows():
        for copy in sum(noisy + other_noisy, []) + sum(wide, []):
            copy.wait_recv()
        for copy in back:
            copy.wait()
        pulls = [
            pltpu.make_async_copy(src, dst, load_sem.at[i])
            for i, (src, dst) in enumerate(
                ((qg, q_all), (dog, do_all), (kn, keys.at[0:span]), (vn, values.at[0:span]))
            )
        ]
        for copy in pulls:
            copy.start()
        for copy in pulls:
            copy.wait()
        for r in range(heads):
            at, col = slice(r * rows, (r + 1) * rows), slice(r * HEAD_SIZE, (r + 1) * HEAD_SIZE)
            qs[at] = q_all[:, col]
            dos[at] = do_all[:, col]

    rounds = [[(0, 0)]]
    for near in range(1, me.right + 1, 2):
        rounds.append([(w, far) for far in (near + 1, near) for w in (0, 1) if far <= reach[w]])

    def advance(r):
        if r == 0:
            for stride in (2, 1):
                for i in (0, 1):
                    for w in (0, 1):
                        if stride <= reach[w]:
                            hop(w, 0, stride, i)
            pass_on(source(0, 0))
            return
        for begin in range(0, len(rounds[r]), 2):
            group = rounds[r][begin : begin + 2]
            for i in (0, 1):
                for direction, far in group:
                    arriving[direction, far, i].wait_recv()
                    if far + 2 <= reach[direction]:
                        hop(direction, far, 2, i)
            for unit in group:
                p = source(*unit)
                pass_on(p)
                if r == len(rounds) - 1:
                    across[p] = go(
                        remote(kv.at[OWN, p], kv.at[FAR, p], gx_send.at[2, p], gx_recv.at[2, p], me.x_peer(2))
                    )

    def hand_round(r):
        for unit in rounds[r]:
            hand_over(source(*unit))

    advance(0)
    for copy in pair_kv:
        copy.wait_recv()
    other_noisy = [
        spread(6 + i, src, lambda j, dst=dst: dst.at[pl.ds(pl.multiple_of(rows + j * few, 8), few)], kw)
        for i, (src, dst) in enumerate(((kp, kn), (vp, vn)))
    ]
    for i, (src, dst) in enumerate(((kp, own_kp), (vp, own_vp))):
        local.append(pltpu.make_async_copy(src.at[:, lanes(mine, kw)], dst, own_sem.at[6 + i]))
        local[-1].start()
    advance(1)
    for copy in local[2:]:
        copy.wait()
    back = [
        pltpu.make_async_copy(src, dst, own_sem.at[i])
        for i, (src, dst) in enumerate(
            (
                (own_k, kn.at[token_rows(mine)]),
                (own_v, vn.at[token_rows(mine)]),
                (own_q, qg.at[token_rows(mine)]),
                (own_do, dog.at[token_rows(mine)]),
                (own_kp, kn.at[pl.ds(pl.multiple_of(rows + mine * few, 8), few)]),
                (own_vp, vn.at[pl.ds(pl.multiple_of(rows + mine * few, 8), few)]),
            )
        )
    ]
    for copy in back:
        copy.start()
    listing.wait()
    take_rows()
    advance(2)
    hand_round(0)
    listed_rows(OWN, 0)
    score(0)
    hand_round(1)
    advance(3)
    hand_round(2)
    listed_rows(RIGHT, 0)
    listed_rows(LEFT, 0)
    advance(4)
    score(1)
    hand_round(3)
    listed_rows(OWN, 1)
    for p in range(half):
        across[p].wait_recv()
    listed_rows(FAR, 0)
    score(2)
    for unit in rounds[4]:
        for i in (0, 1):
            sideways[source(*unit), i].wait_recv()
    listed_rows(RIGHT, 1)
    listed_rows(LEFT, 1)
    for p in range(half, nz):
        across[p].wait_recv()
    listed_rows(FAR, 1)
    score(3)

    def finish(r):
        at = slice(r * rows, (r + 1) * rows)
        col = slice(r * HEAD_SIZE, (r + 1) * HEAD_SIZE)
        top, inverse = peak[at], 1.0 / jnp.sum(norm[at], -1, keepdims=True)
        o = (acc[at] * inverse).astype(BF16)
        o_all[:, col] = o
        row_dot = jnp.sum(dos[at].astype(F32) * o.astype(F32), -1, keepdims=True)
        for batch, indexes in enumerate(batches):
            factor = jnp.exp2(tops[batch, at] - top) * inverse
            for j in [j for low, count in (chunks[i] for i in indexes) for j in range(low, low + count, HEAD_SIZE)]:
                prob = t[at, j : j + HEAD_SIZE] * factor
                weights[at, j : j + HEAD_SIZE] = prob.astype(BF16)
                dscores[at, j : j + HEAD_SIZE] = (prob * (dp[at, j : j + HEAD_SIZE] - row_dot)).astype(BF16)
        dq_all[:, col] = (dot(dscores[at], keys[...], 1, 0) * SCALE).astype(BF16)

    for r in range(heads):
        finish(r)
    puts = [pltpu.make_async_copy(src, dst, put_sem.at[i]) for i, (src, dst) in enumerate(((o_all, og), (dq_all, dqg)))]
    for copy in puts:
        copy.start()

    def gradients(low, count):
        at = slice(low, low + count)
        return dot(qs[...], dscores[:, at], 0, 0).T * SCALE, dot(dos[...], weights[:, at], 0, 0).T

    def make_terms(side, part):
        for i, g in enumerate(gradients(column(side, part), width)):
            for j in range(half):
                terms[side, part * half + j, i] = g[j * BLK : (j + 1) * BLK].astype(BF16)

    def placed(value, whose, p):
        b = listed[me.wrap_x(whose) * nz + me.z, me.x * nz + me.wrap_z(offsets[p])]
        value = value.astype(F32)
        return jnp.concatenate([jnp.where(b == block, value, 0.0) for block in (0, 1)], 0)

    rounds = []
    for step in range((me.right + 1) // 2):
        rounds.append([(w, reach[w] - 2 * step - i) for i in (0, 1) for w in (0, 1) if reach[w] - 2 * step - i > 0])
    rounds.append([(0, 0)])
    beside, opposite, flying = {}, {}, {}

    def target(direction, far):
        return slot_of[far if direction == 0 else -far]

    def slots(r):
        return [target(*unit) for unit in rounds[r]] if r < len(rounds) else []

    def send_opposite(r):
        for p in slots(r):
            opposite[p] = go(
                remote(terms.at[FAR, p], far_in.at[p], x_send.at[2, p], x_recv.at[2, p], me.x_peer(2))
            )

    def send_beside(r, which=(0, 1)):
        for p in slots(r):
            for i in which:
                side, d = ((RIGHT, 1), (LEFT, -1))[i]
                beside[p, i] = go(
                    remote(terms.at[side, p], side_in.at[i, p], x_send.at[i, p], x_recv.at[i, p], me.x_peer(d))
                )

    def total(direction, far, i):
        p = target(direction, far)
        if i == 0:
            beside[p, 0].wait_recv()
            beside[p, 1].wait_recv()
            opposite[p].wait_recv()
        value = (
            placed(terms[OWN, p, i], 0, p)
            + placed(side_in[0, p, i], -1, p)
            + placed(side_in[1, p, i], 1, p)
            + placed(far_in[p, i], 2, p)
        )
        before = [(direction, far + 2)] if far else [(w, f) for f in (1, 2) for w in (0, 1)]
        for w, f in before:
            if f <= reach[w]:
                flying[w, f, i].wait_recv()
                value = value + ring_in[w, f, i].astype(F32)
        return value.astype(BF16)

    def send_ring(r):
        for begin in range(0, len(rounds[r]), 2):
            group = rounds[r][begin : begin + 2]
            for i in (0, 1):
                for direction, far in group:
                    ring_out[direction, far, i] = total(direction, far, i)
                for direction, far in group:
                    stride = min(2, far)
                    flying[direction, far, i] = go(
                        remote(
                            ring_out.at[direction, far, i], ring_in.at[direction, far, i],
                            z_send.at[direction, far, i], z_recv.at[direction, far, i],
                            me.z_peer(stride if direction == 0 else -stride),
                        )
                    )

    def head_out(which, src_at, dst, size):
        copies = []
        for d in range(1, nh):
            copies.append(
                go(
                    remote(
                        src_at(me.wrap_head(d)), dst.at[:, lanes(mine, size)],
                        out_send.at[which, d], out_recv.at[which, d], me.head_peer(d),
                    )
                )
            )
        return copies

    results = []
    make_terms(FAR, 1)
    send_opposite(0)
    make_terms(RIGHT, 1)
    send_beside(0, (0,))
    make_terms(LEFT, 1)
    send_beside(0, (1,))
    send_opposite(1)
    send_beside(1)
    make_terms(OWN, 1)
    for copy in puts:
        copy.wait()
    mids = [
        pltpu.make_async_copy(og.at[token_rows(mine)], own_q, own_sem.at[0]),
        pltpu.make_async_copy(dqg.at[token_rows(mine)], own_do, own_sem.at[1]),
    ]
    for copy in mids:
        copy.start()
    for i, (src, dst) in enumerate(((og, o_out), (dqg, dq_out))):
        results += head_out(i, lambda j, src=src: src.at[token_rows(j)], dst, qw)
    for i, g in enumerate(gradients(0, span)):
        span_grad[i] = g[0:rows]
        other[i] = g[rows:span].astype(BF16)
    pair = [
        go(remote(other.at[i], pair_in.at[i], pair_send.at[i], pair_recv.at[i], me.partner(mine))) for i in (0, 1)
    ]
    make_terms(FAR, 0)
    make_terms(RIGHT, 0)
    make_terms(LEFT, 0)
    for r in (2, 3, 4):
        send_opposite(r)
        send_beside(r)
    make_terms(OWN, 0)
    send_ring(0)
    for copy in mids:
        copy.wait()
    mids = [
        pltpu.make_async_copy(own_q, o_out.at[:, lanes(mine, qw)], own_sem.at[0]),
        pltpu.make_async_copy(own_do, dq_out.at[:, lanes(mine, qw)], own_sem.at[1]),
    ]
    for copy in mids:
        copy.start()
    for i in (0, 1):
        pair[i].wait_recv()
        noisy_sum[i] = (span_grad[i] + pair_in[i].astype(F32)).astype(BF16)
    put = pltpu.make_async_copy(noisy_sum, ng, put_sem.at[0])
    put.start()
    for r in range(1, len(rounds)):
        if r == len(rounds) - 1:
            break
        send_ring(r)
        if r == 2:
            put.wait()
            tail = [pltpu.make_async_copy(ng.at[i, token_rows(mine)], ref, own_sem.at[2 + i]) for i, ref in enumerate((own_k, own_v))]
            for copy in tail:
                copy.start()
            for i, dst in enumerate((dk_out, dv_out)):
                results += head_out(2 + i, lambda j, i=i: ng.at[i, token_rows(j)], dst, kw)
            for copy in tail:
                copy.wait()
            for i, (ref, dst) in enumerate(((own_k, dk_out), (own_v, dv_out))):
                mids.append(pltpu.make_async_copy(ref, dst.at[:, lanes(mine, kw)], own_sem.at[2 + i]))
                mids[-1].start()
    for i, dst in enumerate((dck_out, dcv_out)):
        final[i] = total(0, 0, i).astype(F32).reshape(final.shape[1:]).astype(BF16)
    for i, dst in enumerate((dck_out, dcv_out)):
        results += head_out(4 + i, lambda j, i=i: final.at[i, j], dst, kw)
        mids.append(pltpu.make_async_copy(final.at[i, mine], dst.at[:, lanes(mine, kw)], own_sem.at[4 + i]))
        mids[-1].start()
    for copy in results:
        copy.wait_recv()
    for copy in sends:
        copy.wait_send()
    for copy in mids:
        copy.wait()


def everything(nz, nh, history, q, do, k, v, ck, cv):
    few, qw, kw, crows = q.shape[0], q.shape[1] // nh, k.shape[1] // nh, ck.shape[0]
    rows = few * nh
    span = 2 * rows
    count = span + NX * nz * BLK
    stacked = rows * (qw // HEAD_SIZE)
    half = nz // 2
    unit = (2, nh, crows, kw)
    dma = pltpu.SemaphoreType.DMA

    def shape(*dims):
        return jax.ShapeDtypeStruct(dims, BF16)

    return pl.pallas_call(
        functools.partial(kernel, nz, nh),
        out_shape=(
            shape(few, nh * qw), shape(few, nh * qw), shape(few, nh * kw), shape(few, nh * kw),
            shape(crows, nh * kw), shape(crows, nh * kw),
            shape(rows, qw), shape(rows, qw), shape(span, kw), shape(span, kw),
            shape(rows, qw), shape(rows, qw), shape(2, rows, kw),
            shape(few, nh * kw), shape(few, nh * kw),
        ),
        in_specs=[ANY] * 7,
        out_specs=(ANY,) * 15,
        scratch_shapes=[
            pltpu.SMEM(history.shape, jnp.int32),
            pltpu.VMEM((NX, nz) + unit, BF16),
            pltpu.VMEM((few, qw), BF16),
            pltpu.VMEM((few, qw), BF16),
            pltpu.VMEM((few, kw), BF16),
            pltpu.VMEM((few, kw), BF16),
            pltpu.VMEM((few, kw), BF16),
            pltpu.VMEM((few, kw), BF16),
            pltpu.VMEM((rows, qw), BF16),
            pltpu.VMEM((rows, qw), BF16),
            pltpu.VMEM((rows, qw), BF16),
            pltpu.VMEM((rows, qw), BF16),
            pltpu.VMEM((stacked, kw), BF16),
            pltpu.VMEM((stacked, kw), BF16),
            pltpu.VMEM((count, kw), BF16),
            pltpu.VMEM((count, kw), BF16),
            pltpu.VMEM((stacked, count), F32),
            pltpu.VMEM((stacked, count), F32),
            pltpu.VMEM((4, stacked, HEAD_SIZE), F32),
            pltpu.VMEM((stacked, HEAD_SIZE), F32),
            pltpu.VMEM((stacked, HEAD_SIZE), F32),
            pltpu.VMEM((stacked, HEAD_SIZE), F32),
            pltpu.VMEM((stacked, count), BF16),
            pltpu.VMEM((stacked, count), BF16),
            pltpu.VMEM((1, count), F32),
            pltpu.VMEM((NX, nz, 2, BLK, kw), BF16),
            pltpu.VMEM((2, nz, 2, BLK, kw), BF16),
            pltpu.VMEM((nz, 2, BLK, kw), BF16),
            pltpu.VMEM((2, half + 1, 2, 2 * BLK, kw), BF16),
            pltpu.VMEM((2, half + 1, 2, 2 * BLK, kw), BF16),
            pltpu.VMEM((2, rows, kw), BF16),
            pltpu.VMEM((2, rows, kw), BF16),
            pltpu.VMEM((2, rows, kw), F32),
            pltpu.VMEM((2, rows, kw), BF16),
            pltpu.VMEM(unit, BF16),
            dma, dma((8, nh)), dma((8, nh)), dma((8,)), dma((4,)),
            dma((2, half + 1, 2)), dma((2, half + 1, 2)), dma((3, nz)), dma((3, nz)),
            dma((6, nh)), dma((6, nh)), dma((2,)), dma((2,)), dma((2,)),
            dma((3, nz)), dma((3, nz)), dma((2, half + 1, 2)), dma((2, half + 1, 2)),
        ],
        compiler_params=pltpu.CompilerParams(
            collective_id=0, has_side_effects=True, vmem_limit_bytes=60 * 2**20
        ),
        name="everything",
    )(history, q, do, k, v, ck, cv)


def settle_kernel(*refs):
    count = len(refs) // 3
    ins, outs, held = refs[:count], refs[count : 2 * count], refs[2 * count : 3 * count]
    sem = refs[3 * count]
    loads = [pltpu.make_async_copy(a, b, sem.at[0, i]) for i, (a, b) in enumerate(zip(ins, held))]
    stores = [pltpu.make_async_copy(a, b, sem.at[1, i]) for i, (a, b) in enumerate(zip(held, outs))]
    for copy in loads:
        copy.start()
    for load, store in zip(loads, stores):
        load.wait()
        store.start()
    for copy in stores:
        copy.wait()


def settle(arrays):
    shapes = [(a.shape, a.dtype) for a in arrays]
    return pl.pallas_call(
        settle_kernel,
        out_shape=tuple(jax.ShapeDtypeStruct(*s) for s in shapes),
        in_specs=[ANY] * len(arrays),
        out_specs=(ANY,) * len(arrays),
        scratch_shapes=[pltpu.VMEM(*s) for s in shapes]
        + [pltpu.SemaphoreType.DMA((2, len(arrays)))] ,
        name="settle",
    )(*arrays)


def shards(nz, nh, queries, nk, nv, ck, cv, output_gradient, history_list):
    results = everything(nz, nh, history_list, queries, output_gradient, nk, nv, ck, cv)
    return settle(results[:6])


def solution(mesh):
    nz, nh = mesh.shape["ctx"] // NX, mesh.shape["head"]
    tokens = P(("ctx", "head"), None)
    return jax.shard_map(
        functools.partial(shards, nz, nh),
        mesh=mesh,
        in_specs=(tokens,) * 6 + (P(),),
        out_specs=(tokens,) * 6,
        check_vma=False,
    )
```
